32 devices in a mesh: shape: 2 (over x), query: 16 (over z, y, core).
Axes of the slice: x: 2, y: 2, z: 4, core: 2. Of those that a mesh axis runs over, the one named last changes fastest.
Arguments:
- latents: bfloat16 [512, 1024], P(('shape', 'query')), parts along dimension 0, may hold values from -6 to 6
- gain_self: float32 [1024], replicated, may hold values from 1.5 to 4, as said below
- w_qkv: bfloat16 [3, 1024, 1024], P(None, 'query'), may hold values from -0.1875 to 0.1875
- w_out: bfloat16 [1024, 1024], P('query'), may hold values from -0.1875 to 0.1875
- gain_cross: float32 [1024], replicated, may hold values from 1.5 to 4, as said below
- w_kv: bfloat16 [2, 1024, 1024], replicated, may hold values from -0.1875 to 0.1875
- w_embed: bfloat16 [51, 1024], replicated, may hold values from -0.875 to 0.875
- gain_point: float32 [1024], replicated, may hold values from 1.5 to 4, as said below
- w_query: bfloat16 [1024, 1024], replicated, may hold values from -0.1875 to 0.1875
- w_back: bfloat16 [1024, 1024], replicated, may hold values from -0.1875 to 0.1875
- gain_head: float32 [1024], replicated, may hold values from 0.5 to 1.5
- w_hidden: bfloat16 [1024, 1024], replicated, may hold values from -0.1875 to 0.1875
- w_sdf: bfloat16 [1024], replicated, may hold values from -0.1875 to 0.1875
Outputs:
- decoded: bfloat16 [512, 1024], P(('shape', 'query')), parts along dimension 0
- sdf: float32 [32768], P(('shape', 'query')), parts along dimension 0
The draws below stay inside these ranges and needn't reach their ends.
There are 2 independent parts, one for each index of `shape`. The reference program is written for one: setup_inputs(seed, part) draws one part's arguments, and reference() takes and returns one part's arrays. A program takes and returns all parts, laid end to end along the dimension named above; an argument that names none is the same for every part. Nothing has to cross between parts.
Inputs may be any that keep to these rules, and one draw needn't show every extreme that they name: `gain_self`: per-channel norm gains. `gain_cross`: per-channel norm gains. `gain_point`: per-channel norm gains.
All inputs are finite; a program needn't handle non-finite values.
Results may differ from the reference program's by a relative error of at most 0.023.
The reference program's roundings to bfloat16 on the way count: a program that leaves them out, or rounds other values in their place, can miss the bound.
Values may be sent and summed in bfloat16 or wider, within the bound.
A program may use at most 128 MiB of HBM per device.

```python
import math
import jax
import jax.numpy as jnp
from jax import lax

D = 1024
HEADS = 16
FREQS = 8
GRID = 512
PTS_DEV = 1024
FE = 51
NLAT = 256
NPTS = 16384
N_QUERY = 16


def gain_law(key):
    return jax.random.uniform(key, (D,), jnp.float32, 1.5, 2.6)


def draw_gain_self(key, part):
    return gain_law(jax.random.fold_in(key, 11))


def draw_gain_cross(key, part):
    return gain_law(jax.random.fold_in(key, 23))


def draw_gain_point(key, part):
    return gain_law(jax.random.fold_in(key, 37))


def level_of(stream_key, dims, shards, smallest, top_value):
    def one(position, parts):
        draws = jax.random.uniform(jax.random.fold_in(jax.random.fold_in(stream_key, 6), position), (parts,), jnp.float32, smallest / len(shards), top_value / len(shards))
        return jnp.repeat(jnp.exp(draws), dims[position] // parts).reshape((-1,) + (1,) * (len(dims) - position - 1))

    level = one(*shards[0])
    for cut in shards[1:]:
        level = level * one(*cut)
    return level


def bell_draw(stream_key, shape, deviation, most, shards=(), kind=jnp.bfloat16):
    drawn = jax.random.normal(stream_key, shape, jnp.float32) * deviation
    if len(shards) > 0:
        drawn = level_of(stream_key, shape, shards, -0.22, 0.18) * drawn
    return jnp.clip(drawn, min=-most, max=most).astype(kind)


def setup_inputs(seed: int = 0, part: int = 0) -> dict:
    key_list = jax.random.split(jax.random.key(seed), 14)
    own_keys = jax.random.split(jax.random.fold_in(key_list[13], part), 14)
    latents = bell_draw(own_keys[0], (NLAT, D), 1.0, 6.0, ((0, 16),))
    gain_self = draw_gain_self(jax.random.fold_in(key_list[13], 71), part)
    w_qkv = bell_draw(key_list[2], (3, D, D), D ** -0.5, 0.1875, ((1, 16),))
    w_out = bell_draw(key_list[3], (D, D), D ** -0.5, 0.1875, ((0, 16),))
    gain_cross = draw_gain_cross(jax.random.fold_in(key_list[13], 71), part)
    w_kv = bell_draw(key_list[5], (2, D, D), D ** -0.5, 0.1875)
    w_embed = bell_draw(key_list[6], (FE, D), FE ** -0.5, 0.875)
    gain_point = draw_gain_point(jax.random.fold_in(key_list[13], 71), part)
    w_query = bell_draw(key_list[8], (D, D), D ** -0.5, 0.1875)
    w_back = bell_draw(key_list[9], (D, D), D ** -0.5, 0.1875)
    gain_head = jnp.clip(1.0 + 0.1 * jax.random.normal(key_list[10], (D,), jnp.float32), 0.5, 1.5)
    w_hidden = bell_draw(key_list[11], (D, D), D ** -0.5, 0.1875)
    w_sdf = bell_draw(key_list[12], (D,), D ** -0.5, 0.1875)
    return {"latents": latents, "gain_self": gain_self, "w_qkv": w_qkv, "w_out": w_out, "gain_cross": gain_cross, "w_kv": w_kv, "w_embed": w_embed, "gain_point": gain_point, "w_query": w_query, "w_back": w_back, "gain_head": gain_head, "w_hidden": w_hidden, "w_sdf": w_sdf}


def norm_rows(values, gain):
    center = lax.optimization_barrier(jnp.mean(values, axis=-1, keepdims=True))
    centred = values - center
    spread = lax.optimization_barrier(jnp.mean(centred * centred, axis=-1, keepdims=True))
    return centred * lax.rsqrt(spread + 1e-05) * gain

def attend(queries, keys, values):
    row_count, features = queries.shape
    key_count = keys.shape[0]
    head_dim = features // HEADS
    group_count = HEADS // 4
    head_queries = queries.reshape(row_count, group_count, 4, head_dim).transpose(1, 0, 2, 3)
    head_keys = keys.reshape(key_count, group_count, 4, head_dim).transpose(1, 0, 2, 3)
    head_values = values.reshape(key_count, group_count, 4, head_dim).transpose(1, 0, 2, 3)
    scaling = 1.0 / math.sqrt(head_dim)

    def per_group(block):
        group_query, group_keys, group_values = block
        scores = jnp.einsum('rge,nge->grn', group_query.astype(jnp.float32), group_keys.astype(jnp.float32)) * scaling
        highest = lax.optimization_barrier(jnp.max(scores, axis=-1, keepdims=True))
        powers = jnp.exp(scores - highest)
        total = lax.optimization_barrier(jnp.sum(powers, axis=-1, keepdims=True))
        weights = (powers / total).astype(jnp.bfloat16)
        blended = jnp.einsum('grn,nge->rge', weights.astype(jnp.float32), group_values.astype(jnp.float32))
        return blended.astype(jnp.bfloat16)
    result = lax.map(per_group, (head_queries, head_keys, head_values))
    return result.transpose(1, 0, 2, 3).reshape(row_count, features)

def point_features(numbers):
    cell_i = numbers // (GRID * GRID)
    cell_j = numbers // GRID % GRID
    cell_k = numbers % GRID
    cells = jnp.stack([cell_i, cell_j, cell_k], axis=1).astype(jnp.float32)
    coords = (2.0 * cells + 1.0) / GRID - 1.0
    freqs = 2.0 ** jnp.arange(FREQS, dtype=jnp.float32) * math.pi
    angles = (coords[:, :, None] * freqs[None, None, :]).reshape(numbers.shape[0], 3 * FREQS)
    return jnp.concatenate([coords, jnp.sin(angles), jnp.cos(angles)], axis=1).astype(jnp.bfloat16)

def decode_points(numbers, keys, values, w_embed, gain_point, w_query, w_back, gain_head, w_hidden, w_sdf):
    features = point_features(numbers)
    embedded = jnp.dot(features, w_embed, preferred_element_type=jnp.float32)
    normed = norm_rows(embedded, gain_point).astype(jnp.bfloat16)
    point_query = jnp.dot(normed, w_query, preferred_element_type=jnp.float32).astype(jnp.bfloat16)
    crossed = attend(point_query, keys, values)
    joined = embedded + jnp.dot(crossed, w_back, preferred_element_type=jnp.float32)
    head_in = norm_rows(joined, gain_head).astype(jnp.bfloat16)
    hidden = jax.nn.gelu(jnp.dot(head_in, w_hidden, preferred_element_type=jnp.float32)).astype(jnp.bfloat16)
    return jnp.dot(hidden, w_sdf, preferred_element_type=jnp.float32)

def reference(latents, gain_self, w_qkv, w_out, gain_cross, w_kv, w_embed, gain_point, w_query, w_back, gain_head, w_hidden, w_sdf):
    inputs = latents.astype(jnp.float32)
    normed = norm_rows(inputs, gain_self).astype(jnp.bfloat16)
    qkv = jnp.einsum('rd,sdc->src', normed.astype(jnp.float32), w_qkv.astype(jnp.float32)).astype(jnp.bfloat16)
    attended = attend(qkv[0], qkv[1], qkv[2])
    decoded = (inputs + jnp.dot(attended, w_out, preferred_element_type=jnp.float32)).astype(jnp.bfloat16)
    normed_two = norm_rows(decoded.astype(jnp.float32), gain_cross).astype(jnp.bfloat16)
    keys_values = jnp.einsum('rd,sdc->src', normed_two.astype(jnp.float32), w_kv.astype(jnp.float32)).astype(jnp.bfloat16)

    def decode_block(block_index):
        numbers = block_index * PTS_DEV + jnp.arange(PTS_DEV, dtype=jnp.int32)
        return decode_points(numbers, keys_values[0], keys_values[1], w_embed, gain_point, w_query, w_back, gain_head, w_hidden, w_sdf)
    sdf = lax.map(decode_block, jnp.arange(N_QUERY, dtype=jnp.int32)).reshape(NPTS)
    return (decoded, sdf)
```

```python
import functools
import math

import jax
import jax.numpy as jnp
from jax import lax
from jax.experimental import pallas as pl
from jax.experimental.pallas import tpu as pltpu
from jax.sharding import PartitionSpec as P

HEADS = 16
FREQS = 8
GRID = 512
PTS_DEV = 1024
TILE = 256
MESH = pl.DeviceIdType.MESH


def norm_rows(values, gain):
    center = jnp.mean(values, axis=-1, keepdims=True)
    centred = values - center
    spread = jnp.mean(centred * centred, axis=-1, keepdims=True)
    return centred * lax.rsqrt(spread + 1e-05) * gain


def dot(a, b):
    return jnp.dot(a, b, preferred_element_type=jnp.float32)


def dot_nt(a, b):
    return lax.dot_general(a, b, (((1,), (1,)), ((), ())), preferred_element_type=jnp.float32)


class Gather:
    def __init__(self, me, slot, own, send_sem, recv_sem):
        self.me, self.slot, self.own = me, slot, own
        self.send_sem, self.recv_sem = send_sem, recv_sem
        self.z, self.y, self.c = me // 4, (me // 2) % 2, me % 2
        self.sent = []

    def index(self, z, y, c):
        return z * 4 + y * 2 + c

    def send(self, chunk, src, target, number, cond=None):
        copy = pltpu.make_async_remote_copy(
            src_ref=src,
            dst_ref=self.slot(chunk),
            send_sem=self.send_sem.at[number],
            recv_sem=self.recv_sem.at[chunk],
            device_id={"query": target},
            device_id_type=MESH,
        )
        self.sent.append((copy, cond))
        if cond is None:
            copy.start()
        else:
            pl.when(cond)(copy.start)

    def arrived(self, chunk):
        pltpu.make_async_remote_copy(
            src_ref=self.slot(chunk),
            dst_ref=self.slot(chunk),
            send_sem=self.send_sem.at[0],
            recv_sem=self.recv_sem.at[chunk],
            device_id={"query": self.me},
            device_id_type=MESH,
        ).wait_recv()

    def begin(self):
        z, y, c = self.z, self.y, self.c
        self.send(self.me, self.own, self.index(jnp.minimum(z + 1, 3), y, c), 0, z < 3)
        self.send(self.me, self.own, self.index(jnp.maximum(z - 1, 0), y, c), 1, z > 0)
        self.send(self.me, self.own, self.index(z, 1 - y, c), 2)
        self.send(self.me, self.own, self.index(z, y, 1 - c), 3)

    def relay(self, j):
        z, y, c = self.z, self.y, self.c
        for side, (there, onward, nearer) in enumerate(
            ((z - j, z + 1, z - j >= 0), (z + j, z - 1, z + j <= 3))
        ):
            chunk = self.index(jnp.clip(there, 0, 3), y, c)
            pl.when(nearer)(functools.partial(self.arrived, chunk))
            number = 4 + 3 * (2 * (j - 1) + side)
            if j < 3:
                further = jnp.logical_and(nearer, onward <= 3 if side == 0 else onward >= 0)
                self.send(chunk, self.slot(chunk), self.index(jnp.clip(onward, 0, 3), y, c), number, further)
            self.send(chunk, self.slot(chunk), self.index(z, 1 - y, c), number + 1, nearer)
            self.send(chunk, self.slot(chunk), self.index(z, y, 1 - c), number + 2, nearer)

    def across(self):
        for k in range(4):
            chunk = self.index((self.z + k) % 4, 1 - self.y, self.c)
            self.arrived(chunk)
            self.send(chunk, self.slot(chunk), self.index(self.z, self.y, 1 - self.c), 22 + k)

    def finish(self):
        for k in range(4):
            for y in range(2):
                self.arrived(self.index((self.z + k) % 4, y, 1 - self.c))

    def drain(self):
        for copy, cond in self.sent:
            if cond is None:
                copy.wait_send()
            else:
                pl.when(cond)(copy.wait_send)


def latent_kernel(
    n, lat_ref, gain_ref, wqkv_ref, wout_ref,
    lat_all, att_all, wout_all,
    wbuf, normed, lat_send, lat_recv, att_send, att_recv, out_send, out_recv,
    w_send, w_recv, fwd_send, fwd_recv, own_sem,
):
    me = lax.axis_index("query")
    pair, core = me // 2, me % 2
    other = pair * 2 + 1 - core
    rows = lat_ref.shape[0]
    depth = wqkv_ref.shape[1]
    half = depth // 2
    many = lat_all.shape[0]
    qrows = many // 2

    barrier = pltpu.get_barrier_semaphore()
    for k in range(1, n):
        pl.semaphore_signal(barrier, inc=1, device_id={"query": (me + k) % n}, device_id_type=MESH)
    pl.semaphore_wait(barrier, n - 1)

    lat = Gather(me, lambda s: lat_all.at[pl.ds(pl.multiple_of(s * rows, rows), rows), :], lat_ref, lat_send, lat_recv)
    lat.begin()

    def lanes(p):
        return pl.ds(pl.multiple_of(p * 128, 128), 128)

    def wrows(start, size):
        return wbuf.at[:, pl.ds(pl.multiple_of(start, half), size), :]

    copies = []

    def push(src, dst, ssem, rsem, target):
        copy = pltpu.make_async_remote_copy(
            src_ref=src, dst_ref=dst, send_sem=ssem, recv_sem=rsem,
            device_id={"query": target}, device_id_type=MESH,
        )
        copy.start()
        copies.append(copy)

    for k in range(1, n // 2):
        to = (pair + k) % (n // 2)
        for c in range(2):
            push(
                wqkv_ref.at[:, pl.ds(c * half, half), lanes(to)], wrows(me * depth + c * half, half),
                w_send.at[2 * k + c], w_recv.at[me], to * 2 + c,
            )
    push(wqkv_ref.at[:, :, lanes(pair)], wrows(me * depth, depth), w_send.at[0], w_recv.at[me], other)
    mine = pltpu.make_async_copy(wqkv_ref.at[:, :, lanes(pair)], wrows(me * depth, depth), own_sem)
    mine.start()
    out = Gather(me, lambda s: wout_all.at[pl.ds(pl.multiple_of(s * depth, depth), depth), :], wout_ref, out_send, out_recv)
    out.begin()

    lat_all[pl.ds(pl.multiple_of(me * rows, rows), rows), :] = lat_ref[...]
    wout_all[pl.ds(pl.multiple_of(me * depth, depth), depth), :] = wout_ref[...]

    lat.relay(1)
    lat.relay(2)
    lat.relay(3)
    lat.across()
    lat.finish()
    normed[...] = norm_rows(lat_all[...].astype(jnp.float32), gain_ref[...]).astype(jnp.bfloat16)

    def landed(ref, rsem):
        pltpu.make_async_remote_copy(
            src_ref=ref, dst_ref=ref, send_sem=w_send.at[0], recv_sem=rsem,
            device_id={"query": me}, device_id_type=MESH,
        ).wait_recv()

    out.relay(1)
    for k in range(1, n // 2):
        for c in range(2):
            s = ((pair + n // 2 - k) % (n // 2)) * 2 + c
            block = wrows(s * depth + core * half, half)
            landed(block, w_recv.at[s])
            push(block, block, fwd_send.at[2 * k + c], fwd_recv.at[s], other)
    out.relay(2)
    mine.wait()
    landed(wrows(other * depth, depth), w_recv.at[other])
    for k in range(1, n // 2):
        for c in range(2):
            s = ((pair + n // 2 - k) % (n // 2)) * 2 + c
            landed(wrows(s * depth + (1 - core) * half, half), fwd_recv.at[s])

    keys = dot(normed[...], wbuf[1]).astype(jnp.bfloat16)
    values = dot(normed[...], wbuf[2]).astype(jnp.bfloat16)
    part = normed[pl.ds(pl.multiple_of(core * qrows, qrows), qrows), :]
    queries = (dot(part, wbuf[0]).astype(jnp.bfloat16) * 0.125).astype(jnp.bfloat16)
    low = lax.broadcasted_iota(jnp.int32, (qrows, 128), 1) < 64
    outs = []
    for h in range(2):
        masked = jnp.where(low if h == 0 else jnp.logical_not(low), queries, jnp.zeros_like(queries))
        scores = dot_nt(masked, keys)
        powers = jnp.exp(scores - jnp.max(scores, axis=-1, keepdims=True))
        total = jnp.sum(powers, axis=-1, keepdims=True)
        outs.append(dot((powers / total).astype(jnp.bfloat16), values))
    att_all[pair, pl.ds(pl.multiple_of(core * qrows, qrows), qrows), :] = jnp.where(low, outs[0], outs[1]).astype(jnp.bfloat16)

    def att_slot(s):
        return att_all.at[s // 2, pl.ds(pl.multiple_of((s % 2) * qrows, qrows), qrows), :]

    att = Gather(me, att_slot, att_slot(me), att_send, att_recv)
    att.begin()
    out.relay(3)
    out.across()
    att.relay(1)
    att.relay(2)
    att.relay(3)
    att.across()
    out.finish()
    att.finish()
    for copy in copies:
        copy.wait_send()
    lat.drain()
    out.drain()
    att.drain()


def latent_stage(n, latents, gain, w_qkv, w_out):
    many = latents.shape[0] * n
    depth, width = w_out.shape
    vmem = pl.BlockSpec(memory_space=pltpu.VMEM)
    dma = pltpu.SemaphoreType.DMA
    return pl.pallas_call(
        functools.partial(latent_kernel, n),
        out_shape=(
            jax.ShapeDtypeStruct((many, width), jnp.bfloat16),
            jax.ShapeDtypeStruct((n // 2, many, 128), jnp.bfloat16),
            jax.ShapeDtypeStruct((width, width), jnp.bfloat16),
        ),
        in_specs=[vmem] * 4,
        out_specs=(vmem,) * 3,
        scratch_shapes=[
            pltpu.VMEM((3, width, 128), jnp.bfloat16),
            pltpu.VMEM((many, width), jnp.bfloat16),
            dma((26,)), dma((n,)), dma((26,)), dma((n,)), dma((26,)), dma((n,)),
            dma((n,)), dma((n,)), dma((n,)), dma((n,)), dma,
        ],
        compiler_params=pltpu.CompilerParams(collective_id=0, has_side_effects=True),
    )(latents, gain, w_qkv, w_out)


def sin_pi(t):
    r = t - 2.0 * jnp.round(t * 0.5)
    r = jnp.where(r > 0.5, 1.0 - r, jnp.where(r < -0.5, -1.0 - r, r))
    x = r * math.pi
    u = x * x
    series = -1.0 / 39916800.0
    for term in (1.0 / 362880.0, -1.0 / 5040.0, 1.0 / 120.0, -1.0 / 6.0):
        series = series * u + term
    return x + x * u * series


def tile_features(first):
    number = first + lax.broadcasted_iota(jnp.int32, (TILE, 128), 0)
    lane = lax.broadcasted_iota(jnp.int32, (TILE, 128), 1)
    is_coord = lane < 3
    is_cos = lane >= 3 + 3 * FREQS
    rest = jnp.where(is_cos, lane - (3 + 3 * FREQS), lane - 3)
    axis = jnp.where(is_coord, lane, lax.shift_right_arithmetic(rest, 3))
    freq = jnp.where(is_coord, 0, jnp.bitwise_and(rest, 7))
    cell_i = lax.shift_right_arithmetic(number, 18)
    cell_j = jnp.bitwise_and(lax.shift_right_arithmetic(number, 9), GRID - 1)
    cell_k = jnp.bitwise_and(number, GRID - 1)
    cell = jnp.where(axis == 0, cell_i, jnp.where(axis == 1, cell_j, cell_k))
    coord = (2.0 * cell.astype(jnp.float32) + 1.0) / GRID - 1.0
    scale = lax.shift_left(jnp.ones_like(freq), freq).astype(jnp.float32)
    wave = sin_pi(coord * scale + jnp.where(is_cos, 0.5, 0.0))
    feature = jnp.where(is_coord, coord, wave)
    return jnp.where(lane < 3 + 6 * FREQS, feature, 0.0).astype(jnp.bfloat16)


def gelu(x):
    return 0.5 * x * (1.0 + jnp.tanh(math.sqrt(2.0 / math.pi) * (x + 0.044715 * (x * x * x))))


def point_kernel(
    me_ref, lat_ref, att_ref, wout_ref, gcross_ref, wkv_ref, wembed_ref, gpoint_ref,
    wquery_ref, wback_ref, ghead_ref, whidden_ref, wsdf_ref,
    dec_ref, sdf_ref, dec_all, kbd, vext, crossed,
):
    step = pl.program_id(0)
    me = me_ref[0]
    pairs, many, _ = att_ref.shape

    @pl.when(step == 0)
    def _():
        attended = jnp.concatenate([att_ref[p] for p in range(pairs)], axis=1)
        decoded = (lat_ref[...].astype(jnp.float32) + dot(attended, wout_ref[...])).astype(jnp.bfloat16)
        dec_all[...] = decoded
        rows = dec_ref.shape[0]
        dec_ref[...] = dec_all[pl.ds(pl.multiple_of(me * rows, rows), rows), :]
        normed = norm_rows(decoded.astype(jnp.float32), gcross_ref[...]).astype(jnp.bfloat16)
        keys = dot(normed, wkv_ref[0]).astype(jnp.bfloat16).T
        values = dot(normed, wkv_ref[1]).astype(jnp.bfloat16)
        zero = jnp.zeros((64, many), jnp.bfloat16)
        for p in range(pairs):
            kbd[p, :64, :many] = keys[128 * p : 128 * p + 64, :]
            kbd[p, :64, many:] = zero
            kbd[p, 64:, :many] = zero
            kbd[p, 64:, many:] = keys[128 * p + 64 : 128 * p + 128, :]
            vext[p, :, :128] = values[:, 128 * p : 128 * p + 128]
            vext[p, :, 128:] = jnp.ones((many, 128), jnp.bfloat16)

    features = tile_features(me * PTS_DEV + step * TILE)
    embedded = dot(features, wembed_ref[...])
    normed = norm_rows(embedded, gpoint_ref[...]).astype(jnp.bfloat16)
    queries = (dot(normed, wquery_ref[...]).astype(jnp.bfloat16) * 0.125).astype(jnp.bfloat16)
    low = lax.broadcasted_iota(jnp.int32, (TILE, 128), 1) < 64
    for p in range(pairs):
        scores = dot(queries[:, 128 * p : 128 * p + 128], kbd[p])
        outs = []
        for h in range(2):
            s = scores[:, many * h : many * (h + 1)]
            powers = jnp.exp(s - jnp.max(s, axis=-1, keepdims=True)).astype(jnp.bfloat16)
            blended = dot(powers, vext[p])
            outs.append(blended[:, :128] / blended[:, 128:])
        crossed[:, 128 * p : 128 * p + 128] = jnp.where(low, outs[0], outs[1]).astype(jnp.bfloat16)
    joined = embedded + dot(crossed[...], wback_ref[...])
    head_in = norm_rows(joined, ghead_ref[...]).astype(jnp.bfloat16)
    hidden = gelu(dot(head_in, whidden_ref[...])).astype(jnp.bfloat16)
    sdf_ref[...] = dot_nt(wsdf_ref[...], hidden)


def point_stage(me, rows, lat_all, att_all, wout_all, gcross, w_kv, w_embed, gpoint, w_query, w_back, ghead, w_hidden, w_sdf):
    pairs, many, _ = att_all.shape
    width = w_query.shape[0]
    operands = (
        me.reshape(1), lat_all, att_all, wout_all, gcross.reshape(1, -1), w_kv,
        jnp.pad(w_embed, ((0, 128 - w_embed.shape[0]), (0, 0))), gpoint.reshape(1, -1),
        w_query, w_back, ghead.reshape(1, -1), w_hidden, w_sdf.reshape(1, -1),
    )

    def whole(x):
        return pl.BlockSpec(x.shape, lambda i, d=x.ndim: (0,) * d, pipeline_mode=pl.Buffered(1))

    specs = [pl.BlockSpec(memory_space=pltpu.SMEM)] + [whole(x) for x in operands[1:]]
    decoded, sdf = pl.pallas_call(
        point_kernel,
        grid=(PTS_DEV // TILE,),
        out_shape=(
            jax.ShapeDtypeStruct((rows, width), jnp.bfloat16),
            jax.ShapeDtypeStruct((1, PTS_DEV), jnp.float32),
        ),
        in_specs=specs,
        out_specs=(
            pl.BlockSpec((rows, width), lambda i: (0, 0)),
            pl.BlockSpec((1, TILE), lambda i: (0, i)),
        ),
        scratch_shapes=[
            pltpu.VMEM((many, width), jnp.bfloat16),
            pltpu.VMEM((pairs, 128, 2 * many), jnp.bfloat16),
            pltpu.VMEM((pairs, many, 256), jnp.bfloat16),
            pltpu.VMEM((TILE, width), jnp.bfloat16),
        ],
    )(*operands)
    return decoded, sdf.reshape(PTS_DEV)


def attend_all(queries, keys, values):
    rows, width = queries.shape
    head_dim = width // HEADS
    q = queries.reshape(rows, HEADS, head_dim)
    k = keys.reshape(-1, HEADS, head_dim)
    v = values.reshape(-1, HEADS, head_dim)
    scores = jnp.einsum("rhe,nhe->hrn", q, k, preferred_element_type=jnp.float32) / math.sqrt(head_dim)
    weights = jax.nn.softmax(scores, axis=-1).astype(jnp.bfloat16)
    out = jnp.einsum("hrn,nhe->rhe", weights, v, preferred_element_type=jnp.float32)
    return out.astype(jnp.bfloat16).reshape(rows, width)


def latent_stage_gathers(latents, gain, w_qkv, w_out):
    normed = norm_rows(latents.astype(jnp.float32), gain).astype(jnp.bfloat16)
    weights = lax.all_gather(w_qkv, "query", axis=1, tiled=True)
    qkv = jnp.einsum("rd,sdc->src", normed, weights, preferred_element_type=jnp.float32).astype(jnp.bfloat16)
    keys = lax.all_gather(qkv[1], "query", axis=0, tiled=True)
    values = lax.all_gather(qkv[2], "query", axis=0, tiled=True)
    attended = lax.all_gather(attend_all(qkv[0], keys, values), "query", axis=0, tiled=True)
    pairs = attended.shape[1] // 128
    return (
        lax.all_gather(latents, "query", axis=0, tiled=True),
        attended.reshape(-1, pairs, 128).transpose(1, 0, 2),
        lax.all_gather(w_out, "query", axis=0, tiled=True),
    )


def shards(
    n, latents, gain_self, w_qkv, w_out, gain_cross, w_kv, w_embed, gain_point,
    w_query, w_back, gain_head, w_hidden, w_sdf,
):
    me = lax.axis_index("query").astype(jnp.int32)
    if n == HEADS:
        gathered = latent_stage(n, latents, gain_self.reshape(1, -1), w_qkv, w_out)
    else:
        gathered = latent_stage_gathers(latents, gain_self, w_qkv, w_out)
    return point_stage(
        me, latents.shape[0], *gathered, gain_cross, w_kv, w_embed, gain_point,
        w_query, w_back, gain_head, w_hidden, w_sdf,
    )


def solution(mesh):
    return jax.shard_map(
        functools.partial(shards, mesh.shape["query"]),
        mesh=mesh,
        in_specs=(
            P(("shape", "query"), None),
            P(),
            P(None, "query", None),
            P("query", None),
            P(),
            P(),
            P(),
            P(),
            P(),
            P(),
            P(),
            P(),
            P(),
        ),
        out_specs=(P(("shape", "query"), None), P(("shape", "query"))),
        check_vma=False,
    )
```

```python
import functools
import math

import jax
import jax.numpy as jnp
from jax import lax
from jax.experimental import pallas as pl
from jax.experimental.pallas import tpu as pltpu
from jax.sharding import PartitionSpec as P

HEADS = 16
FREQS = 8
GRID = 512
PTS_DEV = 1024
TILE = 256
MESH = pl.DeviceIdType.MESH


def norm_rows(values, gain):
    center = jnp.mean(values, axis=-1, keepdims=True)
    centred = values - center
    spread = jnp.mean(centred * centred, axis=-1, keepdims=True)
    return centred * lax.rsqrt(spread + 1e-05) * gain


def dot(a, b):
    return jnp.dot(a, b, preferred_element_type=jnp.float32)


def dot_nt(a, b):
    return lax.dot_general(a, b, (((1,), (1,)), ((), ())), preferred_element_type=jnp.float32)


class Gather:
    def __init__(self, me, slot, own, send_sem, recv_sem):
        self.me, self.slot, self.own = me, slot, own
        self.send_sem, self.recv_sem = send_sem, recv_sem
        self.z, self.y, self.c = me // 4, (me // 2) % 2, me % 2
        self.sent = []

    def index(self, z, y, c):
        return z * 4 + y * 2 + c

    def send(self, chunk, src, target, number, cond=None):
        copy = pltpu.make_async_remote_copy(
            src_ref=src,
            dst_ref=self.slot(chunk),
            send_sem=self.send_sem.at[number],
            recv_sem=self.recv_sem.at[chunk],
            device_id={"query": target},
            device_id_type=MESH,
        )
        self.sent.append((copy, cond))
        if cond is None:
            copy.start()
        else:
            pl.when(cond)(copy.start)

    def arrived(self, chunk):
        pltpu.make_async_remote_copy(
            src_ref=self.slot(chunk),
            dst_ref=self.slot(chunk),
            send_sem=self.send_sem.at[0],
            recv_sem=self.recv_sem.at[chunk],
            device_id={"query": self.me},
            device_id_type=MESH,
        ).wait_recv()

    def begin(self):
        z, y, c = self.z, self.y, self.c
        self.send(self.me, self.own, self.index(jnp.minimum(z + 1, 3), y, c), 0, z < 3)
        self.send(self.me, self.own, self.index(jnp.maximum(z - 1, 0), y, c), 1, z > 0)
        self.send(self.me, self.own, self.index(z, 1 - y, c), 2)
        self.send(self.me, self.own, self.index(z, y, 1 - c), 3)

    def relay(self, j):
        z, y, c = self.z, self.y, self.c
        for side, (there, onward, nearer) in enumerate(
            ((z - j, z + 1, z - j >= 0), (z + j, z - 1, z + j <= 3))
        ):
            chunk = self.index(jnp.clip(there, 0, 3), y, c)
            pl.when(nearer)(functools.partial(self.arrived, chunk))
            number = 4 + 3 * (2 * (j - 1) + side)
            if j < 3:
                further = jnp.logical_and(nearer, onward <= 3 if side == 0 else onward >= 0)
                self.send(chunk, self.slot(chunk), self.index(jnp.clip(onward, 0, 3), y, c), number, further)
            self.send(chunk, self.slot(chunk), self.index(z, 1 - y, c), number + 1, nearer)
            self.send(chunk, self.slot(chunk), self.index(z, y, 1 - c), number + 2, nearer)

    def across(self):
        for k in range(4):
            chunk = self.index((self.z + k) % 4, 1 - self.y, self.c)
            self.arrived(chunk)
            self.send(chunk, self.slot(chunk), self.index(self.z, self.y, 1 - self.c), 22 + k)

    def finish(self):
        for k in range(4):
            for y in range(2):
                self.arrived(self.index((self.z + k) % 4, y, 1 - self.c))

    def drain(self):
        for copy, cond in self.sent:
            if cond is None:
                copy.wait_send()
            else:
                pl.when(cond)(copy.wait_send)


class DirectGather(Gather):
    def begin(self):
        z, y, c = self.z, self.y, self.c
        for k in (2, 1, 3):
            self.send(self.me, self.own, self.index((z + k) % 4, y, c), k)
        self.send(self.me, self.own, self.index(z, 1 - y, c), 0)
        self.send(self.me, self.own, self.index(z, y, 1 - c), 4)

    def relay(self):
        z, y, c = self.z, self.y, self.c
        for k in (1, 3, 2):
            chunk = self.index((z + k) % 4, y, c)
            self.arrived(chunk)
            self.send(chunk, self.slot(chunk), self.index(z, 1 - y, c), 5 + k)
            self.send(chunk, self.slot(chunk), self.index(z, y, 1 - c), 9 + k)


def sin_pi(t):
    r = t - 2.0 * jnp.round(t * 0.5)
    r = jnp.where(r > 0.5, 1.0 - r, jnp.where(r < -0.5, -1.0 - r, r))
    x = r * math.pi
    u = x * x
    series = -1.0 / 39916800.0
    for term in (1.0 / 362880.0, -1.0 / 5040.0, 1.0 / 120.0, -1.0 / 6.0):
        series = series * u + term
    return x + x * u * series


def tile_features(first):
    number = first + lax.broadcasted_iota(jnp.int32, (TILE, 128), 0)
    lane = lax.broadcasted_iota(jnp.int32, (TILE, 128), 1)
    is_coord = lane < 3
    is_cos = lane >= 3 + 3 * FREQS
    rest = jnp.where(is_cos, lane - (3 + 3 * FREQS), lane - 3)
    axis = jnp.where(is_coord, lane, lax.shift_right_arithmetic(rest, 3))
    freq = jnp.where(is_coord, 0, jnp.bitwise_and(rest, 7))
    cell_i = lax.shift_right_arithmetic(number, 18)
    cell_j = jnp.bitwise_and(lax.shift_right_arithmetic(number, 9), GRID - 1)
    cell_k = jnp.bitwise_and(number, GRID - 1)
    cell = jnp.where(axis == 0, cell_i, jnp.where(axis == 1, cell_j, cell_k))
    coord = (2.0 * cell.astype(jnp.float32) + 1.0) / GRID - 1.0
    scale = lax.shift_left(jnp.ones_like(freq), freq).astype(jnp.float32)
    wave = sin_pi(coord * scale + jnp.where(is_cos, 0.5, 0.0))
    feature = jnp.where(is_coord, coord, wave)
    return jnp.where(lane < 3 + 6 * FREQS, feature, 0.0).astype(jnp.bfloat16)


def gelu(x):
    return 0.5 * x * (1.0 + jnp.tanh(math.sqrt(2.0 / math.pi) * (x + 0.044715 * (x * x * x))))


def whole_kernel(
    n, lat_ref, gself_ref, wqkv_ref, wout_ref, gcross_ref, wembed_ref, gpoint_ref, ghead_ref, wsdf_ref,
    wkv_hbm, wquery_hbm, wback_hbm, whidden_hbm,
    dec_ref, sdf_ref,
    lat_all, att_all, wout_all, wbuf, normed, wkv_ref, wquery_ref, wback_ref, whidden_ref,
    embedded, queries, dec_all, kbd, vext, crossed,
    lat_send, lat_recv, att_send, att_recv, out_send, out_recv,
    w_send, w_recv, fwd_send, fwd_recv, own_sem, load_sem,
):
    me = lax.axis_index("query")
    pair, core = me // 2, me % 2
    other = pair * 2 + 1 - core
    rows = lat_ref.shape[0]
    depth = wqkv_ref.shape[1]
    half = depth // 2
    many = lat_all.shape[0]
    qrows = many // 2
    pairs = n // 2

    loads = [
        pltpu.make_async_copy(src, dst, load_sem.at[i])
        for i, (src, dst) in enumerate(
            ((wquery_hbm, wquery_ref), (wkv_hbm, wkv_ref), (wback_hbm, wback_ref), (whidden_hbm, whidden_ref))
        )
    ]
    for load in loads:
        load.start()

    def pre_tile(t):
        at = slice(t * TILE, (t + 1) * TILE)
        features = tile_features(me * PTS_DEV + t * TILE)
        points = dot(features[:, : wembed_ref.shape[0]], wembed_ref[...])
        embedded[at, :] = points
        ready = norm_rows(points, gpoint_ref[...]).astype(jnp.bfloat16)
        queries[at, :] = (dot(ready, wquery_ref[...]) * 0.125).astype(jnp.bfloat16)

    barrier = pltpu.get_barrier_semaphore()
    for k in range(1, n):
        pl.semaphore_signal(barrier, inc=1, device_id={"query": (me + k) % n}, device_id_type=MESH)
    loads[0].wait()
    pre_tile(0)
    pl.semaphore_wait(barrier, n - 1)

    lat = DirectGather(me, lambda s: lat_all.at[pl.ds(pl.multiple_of(s * rows, rows), rows), :], lat_ref, lat_send, lat_recv)
    lat.begin()

    def lanes(p):
        return pl.ds(pl.multiple_of(p * 128, 128), 128)

    def wrows(start, size):
        return wbuf.at[:, pl.ds(pl.multiple_of(start, half), size), :]

    copies = []

    def push(src, dst, ssem, rsem, target):
        copy = pltpu.make_async_remote_copy(
            src_ref=src, dst_ref=dst, send_sem=ssem, recv_sem=rsem,
            device_id={"query": target}, device_id_type=MESH,
        )
        copy.start()
        copies.append(copy)

    for k in range(1, n // 2):
        to = (pair + k) % (n // 2)
        for c in range(2):
            push(
                wqkv_ref.at[:, pl.ds(c * half, half), lanes(to)], wrows(me * depth + c * half, half),
                w_send.at[2 * k + c], w_recv.at[me], to * 2 + c,
            )
    push(wqkv_ref.at[:, :, lanes(pair)], wrows(me * depth, depth), w_send.at[0], w_recv.at[me], other)
    mine = pltpu.make_async_copy(wqkv_ref.at[:, :, lanes(pair)], wrows(me * depth, depth), own_sem)
    mine.start()
    out = Gather(me, lambda s: wout_all.at[pl.ds(pl.multiple_of(s * depth, depth), depth), :], wout_ref, out_send, out_recv)
    out.begin()

    lat_all[pl.ds(pl.multiple_of(me * rows, rows), rows), :] = lat_ref[...]
    wout_all[pl.ds(pl.multiple_of(me * depth, depth), depth), :] = wout_ref[...]

    pre_tile(1)
    lat.relay()
    lat.across()
    pre_tile(2)
    lat.finish()
    normed[...] = norm_rows(lat_all[...].astype(jnp.float32), gself_ref[...]).astype(jnp.bfloat16)

    def landed(ref, rsem):
        pltpu.make_async_remote_copy(
            src_ref=ref, dst_ref=ref, send_sem=w_send.at[0], recv_sem=rsem,
            device_id={"query": me}, device_id_type=MESH,
        ).wait_recv()

    out.relay(1)
    for k in range(1, pairs):
        for c in range(2):
            s = ((pair + pairs - k) % pairs) * 2 + c
            block = wrows(s * depth + core * half, half)
            landed(block, w_recv.at[s])
            push(block, block, fwd_send.at[2 * k + c], fwd_recv.at[s], other)
    out.relay(2)
    mine.wait()
    landed(wrows(other * depth, depth), w_recv.at[other])
    for k in range(1, pairs):
        for c in range(2):
            s = ((pair + pairs - k) % pairs) * 2 + c
            landed(wrows(s * depth + (1 - core) * half, half), fwd_recv.at[s])

    keys = dot(normed[...], wbuf[1]).astype(jnp.bfloat16)
    values = dot(normed[...], wbuf[2]).astype(jnp.bfloat16)
    part = normed[pl.ds(pl.multiple_of(core * qrows, qrows), qrows), :]
    own_queries = (dot(part, wbuf[0]) * 0.125).astype(jnp.bfloat16)
    low = lax.broadcasted_iota(jnp.int32, (qrows, 128), 1) < 64
    outs = []
    for h in range(2):
        masked = jnp.where(low if h == 0 else jnp.logical_not(low), own_queries, jnp.zeros_like(own_queries))
        scores = dot_nt(masked, keys)
        powers = jnp.exp(scores - jnp.max(scores, axis=-1, keepdims=True))
        total = jnp.sum(powers, axis=-1, keepdims=True)
        outs.append(dot((powers / total).astype(jnp.bfloat16), values))
    att_all[pair, pl.ds(pl.multiple_of(core * qrows, qrows), qrows), :] = jnp.where(low, outs[0], outs[1]).astype(jnp.bfloat16)

    def att_slot(s):
        return att_all.at[s // 2, pl.ds(pl.multiple_of((s % 2) * qrows, qrows), qrows), :]

    att = DirectGather(me, att_slot, att_slot(me), att_send, att_recv)
    att.begin()
    out.relay(3)
    out.across()
    pre_tile(3)
    att.relay()
    att.across()
    out.finish()
    att.finish()

    attended = jnp.concatenate([att_all[p] for p in range(pairs)], axis=1)
    decoded = (lat_all[...].astype(jnp.float32) + dot(attended, wout_all[...])).astype(jnp.bfloat16)
    dec_all[...] = decoded
    dec_ref[...] = dec_all[pl.ds(pl.multiple_of(me * rows, rows), rows), :]
    normed[...] = norm_rows(decoded.astype(jnp.float32), gcross_ref[...]).astype(jnp.bfloat16)
    for load in loads[1:]:
        load.wait()
    cross_keys = dot(normed[...], wkv_ref[0]).astype(jnp.bfloat16).T
    cross_values = dot(normed[...], wkv_ref[1]).astype(jnp.bfloat16)
    zero = jnp.zeros((64, many), jnp.bfloat16)
    for p in range(pairs):
        kbd[p, :64, :many] = cross_keys[128 * p : 128 * p + 64, :]
        kbd[p, :64, many:] = zero
        kbd[p, 64:, :many] = zero
        kbd[p, 64:, many:] = cross_keys[128 * p + 64 : 128 * p + 128, :]
        vext[p, :, :128] = cross_values[:, 128 * p : 128 * p + 128]
        vext[p, :, 128:] = jnp.ones((many, 128), jnp.bfloat16)

    def post_tile(t, carry):
        at = pl.ds(pl.multiple_of(t * TILE, TILE), TILE)
        left = lax.broadcasted_iota(jnp.int32, (TILE, 128), 1) < 64
        for p in range(pairs):
            scores = dot(queries[at, 128 * p : 128 * p + 128], kbd[p])
            parts = []
            for h in range(2):
                s = scores[:, many * h : many * (h + 1)]
                powers = jnp.exp(s - jnp.max(s, axis=-1, keepdims=True)).astype(jnp.bfloat16)
                blended = dot(powers, vext[p])
                parts.append(blended[:, :128] / blended[:, 128:])
            crossed[:, 128 * p : 128 * p + 128] = jnp.where(left, parts[0], parts[1]).astype(jnp.bfloat16)
        joined = embedded[at, :] + dot(crossed[...], wback_ref[...])
        head_in = norm_rows(joined, ghead_ref[...]).astype(jnp.bfloat16)
        hidden = gelu(dot(head_in, whidden_ref[...])).astype(jnp.bfloat16)
        sdf_ref[:, at] = dot_nt(wsdf_ref[...].reshape(1, -1), hidden)
        return carry

    lax.fori_loop(0, PTS_DEV // TILE, post_tile, 0)

    for copy in copies:
        copy.wait_send()
    lat.drain()
    out.drain()
    att.drain()


def shards_kernel(
    n, latents, gain_self, w_qkv, w_out, gain_cross, w_kv, w_embed, gain_point,
    w_query, w_back, gain_head, w_hidden, w_sdf,
):
    rows, width = latents.shape
    many = rows * n
    vmem = pl.BlockSpec(memory_space=pltpu.VMEM)
    anywhere = pl.BlockSpec(memory_space=pl.ANY)
    dma = pltpu.SemaphoreType.DMA
    bf16 = jnp.bfloat16
    decoded, sdf = pl.pallas_call(
        functools.partial(whole_kernel, n),
        out_shape=(
            jax.ShapeDtypeStruct((rows, width), bf16),
            jax.ShapeDtypeStruct((1, PTS_DEV), jnp.float32),
        ),
        in_specs=[vmem] * 9 + [anywhere] * 4,
        out_specs=(vmem,) * 2,
        scratch_shapes=[
            pltpu.VMEM((many, width), bf16),
            pltpu.VMEM((n // 2, many, 128), bf16),
            pltpu.VMEM((width, width), bf16),
            pltpu.VMEM((3, width, 128), bf16),
            pltpu.VMEM((many, width), bf16),
            pltpu.VMEM(w_kv.shape, bf16),
            pltpu.VMEM(w_query.shape, bf16),
            pltpu.VMEM(w_back.shape, bf16),
            pltpu.VMEM(w_hidden.shape, bf16),
            pltpu.VMEM((PTS_DEV, width), jnp.float32),
            pltpu.VMEM((PTS_DEV, width), bf16),
            pltpu.VMEM((many, width), bf16),
            pltpu.VMEM((n // 2, 128, 2 * many), bf16),
            pltpu.VMEM((n // 2, many, 256), bf16),
            pltpu.VMEM((TILE, width), bf16),
            dma((26,)), dma((n,)), dma((26,)), dma((n,)), dma((26,)), dma((n,)),
            dma((n,)), dma((n,)), dma((n,)), dma((n,)), dma, dma((4,)),
        ],
        compiler_params=pltpu.CompilerParams(collective_id=0, has_side_effects=True),
    )(
        latents, gain_self.reshape(1, -1), w_qkv, w_out, gain_cross.reshape(1, -1), w_embed,
        gain_point.reshape(1, -1), gain_head.reshape(1, -1), w_sdf, w_kv, w_query, w_back, w_hidden,
    )
    return decoded, sdf.reshape(PTS_DEV)


def attend(queries, keys, values):
    row_count, features = queries.shape
    key_count = keys.shape[0]
    head_dim = features // HEADS
    group_count = HEADS // 4
    head_queries = queries.reshape(row_count, group_count, 4, head_dim).transpose(1, 0, 2, 3)
    head_keys = keys.reshape(key_count, group_count, 4, head_dim).transpose(1, 0, 2, 3)
    head_values = values.reshape(key_count, group_count, 4, head_dim).transpose(1, 0, 2, 3)
    scaling = 1.0 / math.sqrt(head_dim)

    def per_group(block):
        group_query, group_keys, group_values = block
        scores = (
            jnp.einsum("rge,nge->grn", group_query, group_keys, preferred_element_type=jnp.float32)
            * scaling
        )
        highest = jnp.max(scores, axis=-1, keepdims=True)
        powers = jnp.exp(scores - highest)
        total = jnp.sum(powers, axis=-1, keepdims=True)
        weights = (powers / total).astype(jnp.bfloat16)
        blended = jnp.einsum(
            "grn,nge->rge", weights, group_values, preferred_element_type=jnp.float32
        )
        return blended.astype(jnp.bfloat16)

    result = lax.map(per_group, (head_queries, head_keys, head_values))
    return result.transpose(1, 0, 2, 3).reshape(row_count, features)


def point_features(numbers):
    cell_i = numbers // (GRID * GRID)
    cell_j = numbers // GRID % GRID
    cell_k = numbers % GRID
    cells = jnp.stack([cell_i, cell_j, cell_k], axis=1).astype(jnp.float32)
    coords = (2.0 * cells + 1.0) / GRID - 1.0
    freqs = 2.0 ** jnp.arange(FREQS, dtype=jnp.float32) * math.pi
    angles = (coords[:, :, None] * freqs[None, None, :]).reshape(numbers.shape[0], 3 * FREQS)
    return jnp.concatenate([coords, jnp.sin(angles), jnp.cos(angles)], axis=1).astype(jnp.bfloat16)


def shards_gathers(
    latents,
    gain_self,
    w_qkv,
    w_out,
    gain_cross,
    w_kv,
    w_embed,
    gain_point,
    w_query,
    w_back,
    gain_head,
    w_hidden,
    w_sdf,
):
    inputs = latents.astype(jnp.float32)
    normed = norm_rows(inputs, gain_self).astype(jnp.bfloat16)
    columns = normed
    qkv = jnp.einsum(
        "rd,sdc->src",
        columns,
        lax.all_gather(w_qkv, "query", axis=1, tiled=True),
        preferred_element_type=jnp.float32,
    ).astype(jnp.bfloat16)
    self_keys, self_values = (
        lax.all_gather(qkv[1], "query", axis=0, tiled=True),
        lax.all_gather(qkv[2], "query", axis=0, tiled=True),
    )
    attended = attend(qkv[0], self_keys, self_values)
    columns = attended
    update = jnp.dot(
        columns,
        lax.all_gather(w_out, "query", axis=0, tiled=True),
        preferred_element_type=jnp.float32,
    )
    decoded = (inputs + update).astype(jnp.bfloat16)
    normed_two = norm_rows(decoded.astype(jnp.float32), gain_cross).astype(jnp.bfloat16)
    stacked = jnp.einsum(
        "rd,sdc->src",
        lax.all_gather(normed_two, "query", axis=0, tiled=True),
        w_kv,
        preferred_element_type=jnp.float32,
    ).astype(jnp.bfloat16)
    cross_keys, cross_values = (stacked[0], stacked[1])
    numbers = lax.axis_index("query") * PTS_DEV + jnp.arange(PTS_DEV, dtype=jnp.int32)
    features = point_features(numbers)
    embedded = jnp.dot(features, w_embed, preferred_element_type=jnp.float32)
    point_normed = norm_rows(embedded, gain_point).astype(jnp.bfloat16)
    point_query = jnp.dot(point_normed, w_query, preferred_element_type=jnp.float32).astype(
        jnp.bfloat16
    )
    crossed = attend(point_query, cross_keys, cross_values)
    joined = embedded + jnp.dot(crossed, w_back, preferred_element_type=jnp.float32)
    head_in = norm_rows(joined, gain_head).astype(jnp.bfloat16)
    hidden = jax.nn.gelu(jnp.dot(head_in, w_hidden, preferred_element_type=jnp.float32)).astype(
        jnp.bfloat16
    )
    sdf = jnp.dot(hidden, w_sdf, preferred_element_type=jnp.float32)
    return (decoded, sdf)


def solution(mesh):
    n = mesh.shape["query"]
    body = functools.partial(shards_kernel, n) if n == HEADS else shards_gathers
    return jax.shard_map(
        body,
        mesh=mesh,
        in_specs=(
            P(("shape", "query"), None),
            P(),
            P(None, "query", None),
            P("query", None),
            P(),
            P(),
            P(),
            P(),
            P(),
            P(),
            P(),
            P(),
            P(),
        ),
        out_specs=(P(("shape", "query"), None), P(("shape", "query"))),
        check_vma=False,
    )
```

```python
import functools
import math

import jax
import jax.numpy as jnp
from jax import lax
from jax.experimental import pallas as pl
from jax.experimental.pallas import tpu as pltpu
from jax.sharding import PartitionSpec as P

HEADS = 16
FREQS = 8
GRID = 512
PTS_DEV = 1024
TILE = 256
MESH = pl.DeviceIdType.MESH


def norm_rows(values, gain):
    center = jnp.mean(values, axis=-1, keepdims=True)
    centred = values - center
    spread = jnp.mean(centred * centred, axis=-1, keepdims=True)
    return centred * lax.rsqrt(spread + 1e-05) * gain


def dot(a, b):
    return jnp.dot(a, b, preferred_element_type=jnp.float32)


def dot_nt(a, b):
    return lax.dot_general(a, b, (((1,), (1,)), ((), ())), preferred_element_type=jnp.float32)


class Gather:
    def __init__(self, me, slot, own, send_sem, recv_sem):
        self.me, self.slot, self.own = me, slot, own
        self.send_sem, self.recv_sem = send_sem, recv_sem
        self.z, self.y, self.c = me // 4, (me // 2) % 2, me % 2
        self.sent = []

    def index(self, z, y, c):
        return z * 4 + y * 2 + c

    def send(self, chunk, src, target, number, cond=None):
        copy = pltpu.make_async_remote_copy(
            src_ref=src,
            dst_ref=self.slot(chunk),
            send_sem=self.send_sem.at[number],
            recv_sem=self.recv_sem.at[chunk],
            device_id={"query": target},
            device_id_type=MESH,
        )
        self.sent.append((copy, cond))
        if cond is None:
            copy.start()
        else:
            pl.when(cond)(copy.start)

    def arrived(self, chunk):
        pltpu.make_async_remote_copy(
            src_ref=self.slot(chunk),
            dst_ref=self.slot(chunk),
            send_sem=self.send_sem.at[0],
            recv_sem=self.recv_sem.at[chunk],
            device_id={"query": self.me},
            device_id_type=MESH,
        ).wait_recv()

    def begin(self):
        z, y, c = self.z, self.y, self.c
        self.send(self.me, self.own, self.index(jnp.minimum(z + 1, 3), y, c), 0, z < 3)
        self.send(self.me, self.own, self.index(jnp.maximum(z - 1, 0), y, c), 1, z > 0)
        self.send(self.me, self.own, self.index(z, 1 - y, c), 2)
        self.send(self.me, self.own, self.index(z, y, 1 - c), 3)

    def relay(self, j):
        z, y, c = self.z, self.y, self.c
        for side, (there, onward, nearer) in enumerate(
            ((z - j, z + 1, z - j >= 0), (z + j, z - 1, z + j <= 3))
        ):
            chunk = self.index(jnp.clip(there, 0, 3), y, c)
            pl.when(nearer)(functools.partial(self.arrived, chunk))
            number = 4 + 3 * (2 * (j - 1) + side)
            if j < 3:
                further = jnp.logical_and(nearer, onward <= 3 if side == 0 else onward >= 0)
                self.send(chunk, self.slot(chunk), self.index(jnp.clip(onward, 0, 3), y, c), number, further)
            self.send(chunk, self.slot(chunk), self.index(z, 1 - y, c), number + 1, nearer)
            self.send(chunk, self.slot(chunk), self.index(z, y, 1 - c), number + 2, nearer)

    def across(self):
        for k in range(4):
            chunk = self.index((self.z + k) % 4, 1 - self.y, self.c)
            self.arrived(chunk)
            self.send(chunk, self.slot(chunk), self.index(self.z, self.y, 1 - self.c), 22 + k)

    def finish(self):
        for k in range(4):
            for y in range(2):
                self.arrived(self.index((self.z + k) % 4, y, 1 - self.c))

    def drain(self):
        for copy, cond in self.sent:
            if cond is None:
                copy.wait_send()
            else:
                pl.when(cond)(copy.wait_send)


class DirectGather(Gather):
    def begin(self):
        z, y, c = self.z, self.y, self.c
        for k in (2, 1, 3):
            self.send(self.me, self.own, self.index((z + k) % 4, y, c), k)
        self.send(self.me, self.own, self.index(z, 1 - y, c), 0)
        self.send(self.me, self.own, self.index(z, y, 1 - c), 4)

    def relay(self):
        z, y, c = self.z, self.y, self.c
        for k in (1, 3, 2):
            chunk = self.index((z + k) % 4, y, c)
            self.arrived(chunk)
            self.send(chunk, self.slot(chunk), self.index(z, 1 - y, c), 5 + k)
            self.send(chunk, self.slot(chunk), self.index(z, y, 1 - c), 9 + k)


class SplitGather(Gather):
    def __init__(self, me, plane, slot, rest, own, own_rest, sems):
        super().__init__(me, slot, own, sems[0], sems[1])
        self.plane, self.rest, self.own_rest = plane, rest, own_rest
        self.x_send, self.x_recv, self.s_send, self.s_recv = sems[2:]

    def copy(self, src, dst, send_sem, recv_sem, where, cond=None):
        copy = pltpu.make_async_remote_copy(
            src_ref=src, dst_ref=dst, send_sem=send_sem, recv_sem=recv_sem,
            device_id=where, device_id_type=MESH,
        )
        self.sent.append((copy, cond))
        if cond is None:
            copy.start()
        else:
            pl.when(cond)(copy.start)

    def to_other_shape(self, chunk, number, cond=None):
        where = {"shape": 1 - self.plane, "query": self.me}
        self.copy(self.slot(chunk), self.slot(chunk), self.x_send.at[number], self.x_recv.at[chunk], where, cond)

    def to_core(self, chunk, src, number):
        where = {"query": self.index(self.z, self.y, 1 - self.c)}
        self.copy(src, self.rest(chunk), self.s_send.at[number], self.s_recv.at[chunk], where)

    def rest_arrived(self, chunk, recv_sem):
        pltpu.make_async_remote_copy(
            src_ref=self.rest(chunk), dst_ref=self.rest(chunk), send_sem=self.x_send.at[0],
            recv_sem=recv_sem.at[chunk], device_id={"query": self.me}, device_id_type=MESH,
        ).wait_recv()

    def begin(self):
        super().begin()
        self.to_core(self.me, self.own_rest, 0)

    def relay(self, j):
        super().relay(j)
        z = self.z
        self.to_other_shape(self.index(jnp.maximum(z - j, 0), self.y, self.c), 2 * j - 2, z - j >= 0)
        self.to_other_shape(self.index(jnp.minimum(z + j, 3), self.y, self.c), 2 * j - 1, z + j <= 3)

    def across(self):
        super().across()
        for k in range(4):
            self.to_other_shape(self.index((self.z + k) % 4, 1 - self.y, self.c), 6 + k)

    def collect(self):
        for y, first in ((self.y, 1), (1 - self.y, 0)):
            for k in range(first, 4):
                chunk = self.index((self.z + k) % 4, y, self.c)
                self.rest_arrived(chunk, self.x_recv)
                self.to_core(chunk, self.rest(chunk), 8 - 4 * first + k)

    def finish(self):
        super().finish()
        for k in range(4):
            for y in range(2):
                self.rest_arrived(self.index((self.z + k) % 4, y, 1 - self.c), self.s_recv)


def sin_pi(t):
    r = t - 2.0 * jnp.round(t * 0.5)
    r = jnp.where(r > 0.5, 1.0 - r, jnp.where(r < -0.5, -1.0 - r, r))
    x = r * math.pi
    u = x * x
    series = -1.0 / 39916800.0
    for term in (1.0 / 362880.0, -1.0 / 5040.0, 1.0 / 120.0, -1.0 / 6.0):
        series = series * u + term
    return x + x * u * series


def tile_features(first):
    number = first + lax.broadcasted_iota(jnp.int32, (TILE, 128), 0)
    lane = lax.broadcasted_iota(jnp.int32, (TILE, 128), 1)
    is_coord = lane < 3
    is_cos = lane >= 3 + 3 * FREQS
    rest = jnp.where(is_cos, lane - (3 + 3 * FREQS), lane - 3)
    axis = jnp.where(is_coord, lane, lax.shift_right_arithmetic(rest, 3))
    freq = jnp.where(is_coord, 0, jnp.bitwise_and(rest, 7))
    cell_i = lax.shift_right_arithmetic(number, 18)
    cell_j = jnp.bitwise_and(lax.shift_right_arithmetic(number, 9), GRID - 1)
    cell_k = jnp.bitwise_and(number, GRID - 1)
    cell = jnp.where(axis == 0, cell_i, jnp.where(axis == 1, cell_j, cell_k))
    coord = (2.0 * cell.astype(jnp.float32) + 1.0) / GRID - 1.0
    scale = lax.shift_left(jnp.ones_like(freq), freq).astype(jnp.float32)
    wave = sin_pi(coord * scale + jnp.where(is_cos, 0.5, 0.0))
    feature = jnp.where(is_coord, coord, wave)
    return jnp.where(lane < 3 + 6 * FREQS, feature, 0.0).astype(jnp.bfloat16)


def gelu(x):
    return 0.5 * x * (1.0 + jnp.tanh(math.sqrt(2.0 / math.pi) * (x + 0.044715 * (x * x * x))))


def whole_kernel(
    n, lat_ref, gself_ref, wqkv_ref, wout_ref, gcross_ref, wembed_ref, gpoint_ref, ghead_ref, wsdf_ref,
    wkv_hbm, wquery_hbm, wback_hbm, whidden_hbm,
    dec_ref, sdf_ref,
    lat_all, att_all, wout_all, wbuf, normed, wkv_ref, wquery_ref, wback_ref, whidden_ref,
    embedded, queries, dec_all, kbd, vext, crossed,
    lat_send, lat_recv, att_send, att_recv, out_send, out_recv,
    x_send, x_recv, s_send, s_recv, w_send, w_recv, fwd_send, fwd_recv, own_sem, load_sem,
):
    me = lax.axis_index("query")
    pair, core = me // 2, me % 2
    other = pair * 2 + 1 - core
    rows = lat_ref.shape[0]
    depth = wqkv_ref.shape[1]
    half = depth // 2
    many = lat_all.shape[0]
    qrows = many // 2
    pairs = n // 2

    loads = [
        pltpu.make_async_copy(src, dst, load_sem.at[i])
        for i, (src, dst) in enumerate(
            ((wquery_hbm, wquery_ref), (wkv_hbm, wkv_ref), (wback_hbm, wback_ref), (whidden_hbm, whidden_ref))
        )
    ]
    for load in loads:
        load.start()

    def pre_tile(t):
        at = slice(t * TILE, (t + 1) * TILE)
        features = tile_features(me * PTS_DEV + t * TILE)
        points = dot(features[:, : wembed_ref.shape[0]], wembed_ref[...])
        embedded[at, :] = points
        ready = norm_rows(points, gpoint_ref[...]).astype(jnp.bfloat16)
        queries[at, :] = (dot(ready, wquery_ref[...]) * 0.125).astype(jnp.bfloat16)

    barrier = pltpu.get_barrier_semaphore()
    for k in range(1, n):
        pl.semaphore_signal(barrier, inc=1, device_id={"query": (me + k) % n}, device_id_type=MESH)
    pl.semaphore_signal(
        barrier, inc=1, device_id={"shape": 1 - lax.axis_index("shape"), "query": me}, device_id_type=MESH
    )
    loads[0].wait()
    pre_tile(0)
    pl.semaphore_wait(barrier, n)

    lat = DirectGather(me, lambda s: lat_all.at[pl.ds(pl.multiple_of(s * rows, rows), rows), :], lat_ref, lat_send, lat_recv)
    lat.begin()

    def lanes(p):
        return pl.ds(pl.multiple_of(p * 128, 128), 128)

    def wrows(start, size):
        return wbuf.at[:, pl.ds(pl.multiple_of(start, half), size), :]

    copies = []

    def push(src, dst, ssem, rsem, target):
        copy = pltpu.make_async_remote_copy(
            src_ref=src, dst_ref=dst, send_sem=ssem, recv_sem=rsem,
            device_id={"query": target}, device_id_type=MESH,
        )
        copy.start()
        copies.append(copy)

    for k in range(1, n // 2):
        to = (pair + k) % (n // 2)
        for c in range(2):
            push(
                wqkv_ref.at[:, pl.ds(c * half, half), lanes(to)], wrows(me * depth + c * half, half),
                w_send.at[2 * k + c], w_recv.at[me], to * 2 + c,
            )
    push(wqkv_ref.at[:, :, lanes(pair)], wrows(me * depth, depth), w_send.at[0], w_recv.at[me], other)
    mine = pltpu.make_async_copy(wqkv_ref.at[:, :, lanes(pair)], wrows(me * depth, depth), own_sem)
    mine.start()
    plane = lax.axis_index("shape")

    def out_slot(part, s):
        return wout_all.at[pl.ds(pl.multiple_of(s * depth + part * half, half), half), :]

    def out_own(part):
        return wout_ref.at[pl.ds(pl.multiple_of(part * half, half), half), :]

    out = SplitGather(
        me, plane, functools.partial(out_slot, plane), functools.partial(out_slot, 1 - plane),
        out_own(plane), out_own(1 - plane), (out_send, out_recv, x_send, x_recv, s_send, s_recv),
    )
    out.begin()

    lat_all[pl.ds(pl.multiple_of(me * rows, rows), rows), :] = lat_ref[...]
    wout_all[pl.ds(pl.multiple_of(me * depth, depth), depth), :] = wout_ref[...]

    pre_tile(1)
    lat.relay()
    lat.across()
    pre_tile(2)
    lat.finish()
    normed[...] = norm_rows(lat_all[...].astype(jnp.float32), gself_ref[...]).astype(jnp.bfloat16)

    def landed(ref, rsem):
        pltpu.make_async_remote_copy(
            src_ref=ref, dst_ref=ref, send_sem=w_send.at[0], recv_sem=rsem,
            device_id={"query": me}, device_id_type=MESH,
        ).wait_recv()

    out.relay(1)
    for k in range(1, pairs):
        for c in range(2):
            s = ((pair + pairs - k) % pairs) * 2 + c
            block = wrows(s * depth + core * half, half)
            landed(block, w_recv.at[s])
            push(block, block, fwd_send.at[2 * k + c], fwd_recv.at[s], other)
    out.relay(2)
    mine.wait()
    landed(wrows(other * depth, depth), w_recv.at[other])
    for k in range(1, pairs):
        for c in range(2):
            s = ((pair + pairs - k) % pairs) * 2 + c
            landed(wrows(s * depth + (1 - core) * half, half), fwd_recv.at[s])

    keys = dot(normed[...], wbuf[1]).astype(jnp.bfloat16)
    values = dot(normed[...], wbuf[2]).astype(jnp.bfloat16)
    out.relay(3)
    part = normed[pl.ds(pl.multiple_of(core * qrows, qrows), qrows), :]
    own_queries = (dot(part, wbuf[0]) * 0.125).astype(jnp.bfloat16)
    low = lax.broadcasted_iota(jnp.int32, (qrows, 128), 1) < 64
    outs = []
    for h in range(2):
        masked = jnp.where(low if h == 0 else jnp.logical_not(low), own_queries, jnp.zeros_like(own_queries))
        scores = dot_nt(masked, keys)
        powers = jnp.exp(scores - jnp.max(scores, axis=-1, keepdims=True))
        total = jnp.sum(powers, axis=-1, keepdims=True)
        outs.append(dot((powers / total).astype(jnp.bfloat16), values))
    att_all[pair, pl.ds(pl.multiple_of(core * qrows, qrows), qrows), :] = jnp.where(low, outs[0], outs[1]).astype(jnp.bfloat16)

    def att_slot(s):
        return att_all.at[s // 2, pl.ds(pl.multiple_of((s % 2) * qrows, qrows), qrows), :]

    att = DirectGather(me, att_slot, att_slot(me), att_send, att_recv)
    att.begin()
    out.across()
    pre_tile(3)
    att.relay()
    att.across()
    out.collect()
    out.finish()
    att.finish()

    attended = jnp.concatenate([att_all[p] for p in range(pairs)], axis=1)
    decoded = (lat_all[...].astype(jnp.float32) + dot(attended, wout_all[...])).astype(jnp.bfloat16)
    dec_all[...] = decoded
    dec_ref[...] = dec_all[pl.ds(pl.multiple_of(me * rows, rows), rows), :]
    normed[...] = norm_rows(decoded.astype(jnp.float32), gcross_ref[...]).astype(jnp.bfloat16)
    for load in loads[1:]:
        load.wait()
    cross_keys = dot(normed[...], wkv_ref[0]).astype(jnp.bfloat16).T
    cross_values = dot(normed[...], wkv_ref[1]).astype(jnp.bfloat16)
    zero = jnp.zeros((64, many), jnp.bfloat16)
    for p in range(pairs):
        kbd[p, :64, :many] = cross_keys[128 * p : 128 * p + 64, :]
        kbd[p, :64, many:] = zero
        kbd[p, 64:, :many] = zero
        kbd[p, 64:, many:] = cross_keys[128 * p + 64 : 128 * p + 128, :]
        vext[p, :, :128] = cross_values[:, 128 * p : 128 * p + 128]
        vext[p, :, 128:] = jnp.ones((many, 128), jnp.bfloat16)

    def post_tile(t, carry):
        at = pl.ds(pl.multiple_of(t * TILE, TILE), TILE)
        left = lax.broadcasted_iota(jnp.int32, (TILE, 128), 1) < 64
        for p in range(pairs):
            scores = dot(queries[at, 128 * p : 128 * p + 128], kbd[p])
            parts = []
            for h in range(2):
                s = scores[:, many * h : many * (h + 1)]
                powers = jnp.exp(s - jnp.max(s, axis=-1, keepdims=True)).astype(jnp.bfloat16)
                blended = dot(powers, vext[p])
                parts.append(blended[:, :128] / blended[:, 128:])
            crossed[:, 128 * p : 128 * p + 128] = jnp.where(left, parts[0], parts[1]).astype(jnp.bfloat16)
        joined = embedded[at, :] + dot(crossed[...], wback_ref[...])
        head_in = norm_rows(joined, ghead_ref[...]).astype(jnp.bfloat16)
        hidden = gelu(dot(head_in, whidden_ref[...])).astype(jnp.bfloat16)
        sdf_ref[:, at] = dot_nt(wsdf_ref[...].reshape(1, -1), hidden)
        return carry

    lax.fori_loop(0, PTS_DEV // TILE, post_tile, 0)

    for copy in copies:
        copy.wait_send()
    lat.drain()
    out.drain()
    att.drain()


def shards_kernel(
    n, latents, gain_self, w_qkv, w_out, gain_cross, w_kv, w_embed, gain_point,
    w_query, w_back, gain_head, w_hidden, w_sdf,
):
    rows, width = latents.shape
    many = rows * n
    vmem = pl.BlockSpec(memory_space=pltpu.VMEM)
    anywhere = pl.BlockSpec(memory_space=pl.ANY)
    dma = pltpu.SemaphoreType.DMA
    bf16 = jnp.bfloat16
    decoded, sdf = pl.pallas_call(
        functools.partial(whole_kernel, n),
        out_shape=(
            jax.ShapeDtypeStruct((rows, width), bf16),
            jax.ShapeDtypeStruct((1, PTS_DEV), jnp.float32),
        ),
        in_specs=[vmem] * 9 + [anywhere] * 4,
        out_specs=(vmem,) * 2,
        scratch_shapes=[
            pltpu.VMEM((many, width), bf16),
            pltpu.VMEM((n // 2, many, 128), bf16),
            pltpu.VMEM((width, width), bf16),
            pltpu.VMEM((3, width, 128), bf16),
            pltpu.VMEM((many, width), bf16),
            pltpu.VMEM(w_kv.shape, bf16),
            pltpu.VMEM(w_query.shape, bf16),
            pltpu.VMEM(w_back.shape, bf16),
            pltpu.VMEM(w_hidden.shape, bf16),
            pltpu.VMEM((PTS_DEV, width), jnp.float32),
            pltpu.VMEM((PTS_DEV, width), bf16),
            pltpu.VMEM((many, width), bf16),
            pltpu.VMEM((n // 2, 128, 2 * many), bf16),
            pltpu.VMEM((n // 2, many, 256), bf16),
            pltpu.VMEM((TILE, width), bf16),
            dma((26,)), dma((n,)), dma((26,)), dma((n,)), dma((26,)), dma((n,)),
            dma((n,)), dma((n,)), dma((n,)), dma((n,)), dma((n,)), dma((n,)), dma((n,)), dma((n,)), dma, dma((4,)),
        ],
        compiler_params=pltpu.CompilerParams(collective_id=0, has_side_effects=True),
    )(
        latents, gain_self.reshape(1, -1), w_qkv, w_out, gain_cross.reshape(1, -1), w_embed,
        gain_point.reshape(1, -1), gain_head.reshape(1, -1), w_sdf, w_kv, w_query, w_back, w_hidden,
    )
    return decoded, sdf.reshape(PTS_DEV)


def attend(queries, keys, values):
    row_count, features = queries.shape
    key_count = keys.shape[0]
    head_dim = features // HEADS
    group_count = HEADS // 4
    head_queries = queries.reshape(row_count, group_count, 4, head_dim).transpose(1, 0, 2, 3)
    head_keys = keys.reshape(key_count, group_count, 4, head_dim).transpose(1, 0, 2, 3)
    head_values = values.reshape(key_count, group_count, 4, head_dim).transpose(1, 0, 2, 3)
    scaling = 1.0 / math.sqrt(head_dim)

    def per_group(block):
        group_query, group_keys, group_values = block
        scores = (
            jnp.einsum("rge,nge->grn", group_query, group_keys, preferred_element_type=jnp.float32)
            * scaling
        )
        highest = jnp.max(scores, axis=-1, keepdims=True)
        powers = jnp.exp(scores - highest)
        total = jnp.sum(powers, axis=-1, keepdims=True)
        weights = (powers / total).astype(jnp.bfloat16)
        blended = jnp.einsum(
            "grn,nge->rge", weights, group_values, preferred_element_type=jnp.float32
        )
        return blended.astype(jnp.bfloat16)

    result = lax.map(per_group, (head_queries, head_keys, head_values))
    return result.transpose(1, 0, 2, 3).reshape(row_count, features)


def point_features(numbers):
    cell_i = numbers // (GRID * GRID)
    cell_j = numbers // GRID % GRID
    cell_k = numbers % GRID
    cells = jnp.stack([cell_i, cell_j, cell_k], axis=1).astype(jnp.float32)
    coords = (2.0 * cells + 1.0) / GRID - 1.0
    freqs = 2.0 ** jnp.arange(FREQS, dtype=jnp.float32) * math.pi
    angles = (coords[:, :, None] * freqs[None, None, :]).reshape(numbers.shape[0], 3 * FREQS)
    return jnp.concatenate([coords, jnp.sin(angles), jnp.cos(angles)], axis=1).astype(jnp.bfloat16)


def shards_gathers(
    latents,
    gain_self,
    w_qkv,
    w_out,
    gain_cross,
    w_kv,
    w_embed,
    gain_point,
    w_query,
    w_back,
    gain_head,
    w_hidden,
    w_sdf,
):
    inputs = latents.astype(jnp.float32)
    normed = norm_rows(inputs, gain_self).astype(jnp.bfloat16)
    columns = normed
    qkv = jnp.einsum(
        "rd,sdc->src",
        columns,
        lax.all_gather(w_qkv, "query", axis=1, tiled=True),
        preferred_element_type=jnp.float32,
    ).astype(jnp.bfloat16)
    self_keys, self_values = (
        lax.all_gather(qkv[1], "query", axis=0, tiled=True),
        lax.all_gather(qkv[2], "query", axis=0, tiled=True),
    )
    attended = attend(qkv[0], self_keys, self_values)
    columns = attended
    update = jnp.dot(
        columns,
        lax.all_gather(w_out, "query", axis=0, tiled=True),
        preferred_element_type=jnp.float32,
    )
    decoded = (inputs + update).astype(jnp.bfloat16)
    normed_two = norm_rows(decoded.astype(jnp.float32), gain_cross).astype(jnp.bfloat16)
    stacked = jnp.einsum(
        "rd,sdc->src",
        lax.all_gather(normed_two, "query", axis=0, tiled=True),
        w_kv,
        preferred_element_type=jnp.float32,
    ).astype(jnp.bfloat16)
    cross_keys, cross_values = (stacked[0], stacked[1])
    numbers = lax.axis_index("query") * PTS_DEV + jnp.arange(PTS_DEV, dtype=jnp.int32)
    features = point_features(numbers)
    embedded = jnp.dot(features, w_embed, preferred_element_type=jnp.float32)
    point_normed = norm_rows(embedded, gain_point).astype(jnp.bfloat16)
    point_query = jnp.dot(point_normed, w_query, preferred_element_type=jnp.float32).astype(
        jnp.bfloat16
    )
    crossed = attend(point_query, cross_keys, cross_values)
    joined = embedded + jnp.dot(crossed, w_back, preferred_element_type=jnp.float32)
    head_in = norm_rows(joined, gain_head).astype(jnp.bfloat16)
    hidden = jax.nn.gelu(jnp.dot(head_in, w_hidden, preferred_element_type=jnp.float32)).astype(
        jnp.bfloat16
    )
    sdf = jnp.dot(hidden, w_sdf, preferred_element_type=jnp.float32)
    return (decoded, sdf)


def solution(mesh):
    n = mesh.shape["query"]
    body = functools.partial(shards_kernel, n) if n == HEADS and mesh.shape["shape"] == 2 else shards_gathers
    return jax.shard_map(
        body,
        mesh=mesh,
        in_specs=(
            P(("shape", "query"), None),
            P(),
            P(None, "query", None),
            P("query", None),
            P(),
            P(),
            P(),
            P(),
            P(),
            P(),
            P(),
            P(),
            P(),
        ),
        out_specs=(P(("shape", "query"), None), P(("shape", "query"))),
        check_vma=False,
    )
```

```python
import functools
import math

import jax
import jax.numpy as jnp
from jax import lax
from jax.experimental import pallas as pl
from jax.experimental.pallas import tpu as pltpu
from jax.sharding import PartitionSpec as P

HEADS = 16
FREQS = 8
GRID = 512
PTS_DEV = 1024
TILE = 256
MESH = pl.DeviceIdType.MESH


def norm_rows(values, gain):
    center = jnp.mean(values, axis=-1, keepdims=True)
    centred = values - center
    spread = jnp.mean(centred * centred, axis=-1, keepdims=True)
    return centred * lax.rsqrt(spread + 1e-05) * gain


def dot(a, b):
    return jnp.dot(a, b, preferred_element_type=jnp.float32)


def dot_nt(a, b):
    return lax.dot_general(a, b, (((1,), (1,)), ((), ())), preferred_element_type=jnp.float32)


class Gather:
    def __init__(self, me, slot, own, send_sem, recv_sem):
        self.me, self.slot, self.own = me, slot, own
        self.send_sem, self.recv_sem = send_sem, recv_sem
        self.z, self.y, self.c = me // 4, (me // 2) % 2, me % 2
        self.sent = []

    def index(self, z, y, c):
        return z * 4 + y * 2 + c

    def send(self, chunk, src, target, number, cond=None):
        copy = pltpu.make_async_remote_copy(
            src_ref=src,
            dst_ref=self.slot(chunk),
            send_sem=self.send_sem.at[number],
            recv_sem=self.recv_sem.at[chunk],
            device_id={"query": target},
            device_id_type=MESH,
        )
        self.sent.append((copy, cond))
        if cond is None:
            copy.start()
        else:
            pl.when(cond)(copy.start)

    def arrived(self, chunk):
        pltpu.make_async_remote_copy(
            src_ref=self.slot(chunk),
            dst_ref=self.slot(chunk),
            send_sem=self.send_sem.at[0],
            recv_sem=self.recv_sem.at[chunk],
            device_id={"query": self.me},
            device_id_type=MESH,
        ).wait_recv()

    def begin(self):
        z, y, c = self.z, self.y, self.c
        self.send(self.me, self.own, self.index(jnp.minimum(z + 1, 3), y, c), 0, z < 3)
        self.send(self.me, self.own, self.index(jnp.maximum(z - 1, 0), y, c), 1, z > 0)
        self.send(self.me, self.own, self.index(z, 1 - y, c), 2)
        self.send(self.me, self.own, self.index(z, y, 1 - c), 3)

    def relay(self, j):
        z, y, c = self.z, self.y, self.c
        for side, (there, onward, nearer) in enumerate(
            ((z - j, z + 1, z - j >= 0), (z + j, z - 1, z + j <= 3))
        ):
            chunk = self.index(jnp.clip(there, 0, 3), y, c)
            pl.when(nearer)(functools.partial(self.arrived, chunk))
            number = 4 + 3 * (2 * (j - 1) + side)
            if j < 3:
                further = jnp.logical_and(nearer, onward <= 3 if side == 0 else onward >= 0)
                self.send(chunk, self.slot(chunk), self.index(jnp.clip(onward, 0, 3), y, c), number, further)
            self.send(chunk, self.slot(chunk), self.index(z, 1 - y, c), number + 1, nearer)
            self.send(chunk, self.slot(chunk), self.index(z, y, 1 - c), number + 2, nearer)

    def across(self):
        for k in range(4):
            chunk = self.index((self.z + k) % 4, 1 - self.y, self.c)
            self.arrived(chunk)
            self.send(chunk, self.slot(chunk), self.index(self.z, self.y, 1 - self.c), 22 + k)

    def finish(self):
        for k in range(4):
            for y in range(2):
                self.arrived(self.index((self.z + k) % 4, y, 1 - self.c))

    def drain(self):
        for copy, cond in self.sent:
            if cond is None:
                copy.wait_send()
            else:
                pl.when(cond)(copy.wait_send)


class DirectGather(Gather):
    def begin(self):
        z, y, c = self.z, self.y, self.c
        for k in (2, 1, 3):
            self.send(self.me, self.own, self.index((z + k) % 4, y, c), k)
        self.send(self.me, self.own, self.index(z, 1 - y, c), 0)
        self.send(self.me, self.own, self.index(z, y, 1 - c), 4)

    def relay(self):
        z, y, c = self.z, self.y, self.c
        for k in (1, 3, 2):
            chunk = self.index((z + k) % 4, y, c)
            self.arrived(chunk)
            self.send(chunk, self.slot(chunk), self.index(z, 1 - y, c), 5 + k)
            self.send(chunk, self.slot(chunk), self.index(z, y, 1 - c), 9 + k)


class SplitGather(Gather):
    def __init__(self, me, plane, slot, rest, own, own_rest, sems):
        super().__init__(me, slot, own, sems[0], sems[1])
        self.plane, self.rest, self.own_rest = plane, rest, own_rest
        self.x_send, self.x_recv, self.s_send, self.s_recv = sems[2:]

    def copy(self, src, dst, send_sem, recv_sem, where, cond=None):
        copy = pltpu.make_async_remote_copy(
            src_ref=src, dst_ref=dst, send_sem=send_sem, recv_sem=recv_sem,
            device_id=where, device_id_type=MESH,
        )
        self.sent.append((copy, cond))
        if cond is None:
            copy.start()
        else:
            pl.when(cond)(copy.start)

    def to_other_shape(self, chunk, number, cond=None):
        where = {"shape": 1 - self.plane, "query": self.me}
        self.copy(self.slot(chunk), self.slot(chunk), self.x_send.at[number], self.x_recv.at[chunk], where, cond)

    def to_core(self, chunk, src, number):
        where = {"query": self.index(self.z, self.y, 1 - self.c)}
        self.copy(src, self.rest(chunk), self.s_send.at[number], self.s_recv.at[chunk], where)

    def rest_arrived(self, chunk, recv_sem):
        pltpu.make_async_remote_copy(
            src_ref=self.rest(chunk), dst_ref=self.rest(chunk), send_sem=self.x_send.at[0],
            recv_sem=recv_sem.at[chunk], device_id={"query": self.me}, device_id_type=MESH,
        ).wait_recv()

    def begin(self):
        super().begin()
        self.to_core(self.me, self.own_rest, 0)

    def relay(self, j):
        super().relay(j)
        z = self.z
        self.to_other_shape(self.index(jnp.maximum(z - j, 0), self.y, self.c), 2 * j - 2, z - j >= 0)
        self.to_other_shape(self.index(jnp.minimum(z + j, 3), self.y, self.c), 2 * j - 1, z + j <= 3)

    def across(self):
        super().across()
        for k in range(4):
            self.to_other_shape(self.index((self.z + k) % 4, 1 - self.y, self.c), 6 + k)

    def collect(self):
        for y, first in ((self.y, 1), (1 - self.y, 0)):
            for k in range(first, 4):
                chunk = self.index((self.z + k) % 4, y, self.c)
                self.rest_arrived(chunk, self.x_recv)
                self.to_core(chunk, self.rest(chunk), 8 - 4 * first + k)

    def finish(self):
        super().finish()
        for k in range(4):
            for y in range(2):
                self.rest_arrived(self.index((self.z + k) % 4, y, 1 - self.c), self.s_recv)


def sin_pi(t):
    r = t - 2.0 * jnp.round(t * 0.5)
    r = jnp.where(r > 0.5, 1.0 - r, jnp.where(r < -0.5, -1.0 - r, r))
    x = r * math.pi
    u = x * x
    series = -1.0 / 39916800.0
    for term in (1.0 / 362880.0, -1.0 / 5040.0, 1.0 / 120.0, -1.0 / 6.0):
        series = series * u + term
    return x + x * u * series


def tile_features(first):
    number = first + lax.broadcasted_iota(jnp.int32, (TILE, 128), 0)
    lane = lax.broadcasted_iota(jnp.int32, (TILE, 128), 1)
    is_coord = lane < 3
    is_cos = lane >= 3 + 3 * FREQS
    rest = jnp.where(is_cos, lane - (3 + 3 * FREQS), lane - 3)
    axis = jnp.where(is_coord, lane, lax.shift_right_arithmetic(rest, 3))
    freq = jnp.where(is_coord, 0, jnp.bitwise_and(rest, 7))
    cell_i = lax.shift_right_arithmetic(number, 18)
    cell_j = jnp.bitwise_and(lax.shift_right_arithmetic(number, 9), GRID - 1)
    cell_k = jnp.bitwise_and(number, GRID - 1)
    cell = jnp.where(axis == 0, cell_i, jnp.where(axis == 1, cell_j, cell_k))
    coord = (2.0 * cell.astype(jnp.float32) + 1.0) / GRID - 1.0
    scale = lax.shift_left(jnp.ones_like(freq), freq).astype(jnp.float32)
    wave = sin_pi(coord * scale + jnp.where(is_cos, 0.5, 0.0))
    feature = jnp.where(is_coord, coord, wave)
    return jnp.where(lane < 3 + 6 * FREQS, feature, 0.0).astype(jnp.bfloat16)


def gelu(x):
    return 0.5 * x * (1.0 + jnp.tanh(math.sqrt(2.0 / math.pi) * (x + 0.044715 * (x * x * x))))


def whole_kernel(
    n, lat_ref, gself_ref, wqkv_ref, wout_ref, gcross_ref, wembed_ref, gpoint_ref, ghead_ref, wsdf_ref,
    wkv_hbm, wquery_hbm, wback_hbm, whidden_hbm,
    dec_ref, sdf_ref,
    lat_all, att_all, wout_all, wbuf, normed, wkv_ref, wquery_ref, wback_ref, whidden_ref,
    embedded, queries, dec_all, kbd, vext, crossed,
    lat_send, lat_recv, att_send, att_recv, out_send, out_recv,
    x_send, x_recv, s_send, s_recv, w_send, w_recv, fwd_send, fwd_recv,
    wx_send, wx_recv, last_send, last_recv, own_sem, load_sem,
):
    me = lax.axis_index("query")
    plane = lax.axis_index("shape")
    pair, core = me // 2, me % 2
    other = pair * 2 + 1 - core
    rows = lat_ref.shape[0]
    depth = wqkv_ref.shape[1]
    half = depth // 2
    many = lat_all.shape[0]
    qrows = many // 2
    pairs = n // 2

    loads = [
        pltpu.make_async_copy(src, dst, load_sem.at[i])
        for i, (src, dst) in enumerate(
            ((wquery_hbm, wquery_ref), (wkv_hbm, wkv_ref), (wback_hbm, wback_ref), (whidden_hbm, whidden_ref))
        )
    ]
    for load in loads:
        load.start()

    def pre_tile(t):
        at = slice(t * TILE, (t + 1) * TILE)
        features = tile_features(me * PTS_DEV + t * TILE)
        points = dot(features[:, : wembed_ref.shape[0]], wembed_ref[...])
        embedded[at, :] = points
        ready = norm_rows(points, gpoint_ref[...]).astype(jnp.bfloat16)
        queries[at, :] = (dot(ready, wquery_ref[...]) * 0.125).astype(jnp.bfloat16)

    barrier = pltpu.get_barrier_semaphore()
    for k in range(1, n):
        pl.semaphore_signal(barrier, inc=1, device_id={"query": (me + k) % n}, device_id_type=MESH)
    pl.semaphore_signal(
        barrier, inc=1, device_id={"shape": 1 - plane, "query": me}, device_id_type=MESH
    )
    loads[0].wait()
    pre_tile(0)
    pl.semaphore_wait(barrier, n)

    lat = DirectGather(me, lambda s: lat_all.at[pl.ds(pl.multiple_of(s * rows, rows), rows), :], lat_ref, lat_send, lat_recv)
    lat.begin()

    def lanes(p):
        return pl.ds(pl.multiple_of(p * 128, 128), 128)

    def wrows(start, size):
        return wbuf.at[:, pl.ds(pl.multiple_of(start, half), size), :]

    copies = []

    def push(src, dst, ssem, rsem, target, shape=None):
        copy = pltpu.make_async_remote_copy(
            src_ref=src, dst_ref=dst, send_sem=ssem, recv_sem=rsem,
            device_id={"query": target} if shape is None else {"shape": shape, "query": target},
            device_id_type=MESH,
        )
        copy.start()
        copies.append(copy)

    for k in range(1, pairs):
        to = (pair + k) % pairs
        push(
            wqkv_ref.at[:, pl.ds(pl.multiple_of(plane * half, half), half), lanes(to)],
            wrows(me * depth + plane * half, half), w_send.at[k], w_recv.at[me], to * 2 + core,
        )
    push(wqkv_ref.at[:, :, lanes(pair)], wrows(me * depth, depth), w_send.at[0], w_recv.at[me], other)
    mine = pltpu.make_async_copy(wqkv_ref.at[:, :, lanes(pair)], wrows(me * depth, depth), own_sem)
    mine.start()

    def out_slot(part, s):
        return wout_all.at[pl.ds(pl.multiple_of(s * depth + part * half, half), half), :]

    def out_own(part):
        return wout_ref.at[pl.ds(pl.multiple_of(part * half, half), half), :]

    out = SplitGather(
        me, plane, functools.partial(out_slot, plane), functools.partial(out_slot, 1 - plane),
        out_own(plane), out_own(1 - plane), (out_send, out_recv, x_send, x_recv, s_send, s_recv),
    )
    out.begin()

    lat_all[pl.ds(pl.multiple_of(me * rows, rows), rows), :] = lat_ref[...]
    wout_all[pl.ds(pl.multiple_of(me * depth, depth), depth), :] = wout_ref[...]

    pre_tile(1)
    lat.relay()
    lat.across()
    pre_tile(2)
    lat.finish()
    normed[...] = norm_rows(lat_all[...].astype(jnp.float32), gself_ref[...]).astype(jnp.bfloat16)

    def landed(ref, rsem):
        pltpu.make_async_remote_copy(
            src_ref=ref, dst_ref=ref, send_sem=w_send.at[0], recv_sem=rsem,
            device_id={"query": me}, device_id_type=MESH,
        ).wait_recv()

    out.relay(1)
    for k in range(1, pairs):
        s = ((pair + pairs - k) % pairs) * 2 + core
        block = wrows(s * depth + plane * half, half)
        landed(block, w_recv.at[s])
        push(block, block, wx_send.at[k], wx_recv.at[s], me, 1 - plane)
        push(block, block, fwd_send.at[k], fwd_recv.at[s], other)
    out.relay(2)
    for k in range(1, pairs):
        s = ((pair + pairs - k) % pairs) * 2 + core
        block = wrows(s * depth + (1 - plane) * half, half)
        landed(block, wx_recv.at[s])
        push(block, block, last_send.at[k], last_recv.at[s], other)
    mine.wait()
    landed(wrows(other * depth, depth), w_recv.at[other])
    for k in range(1, pairs):
        s = ((pair + pairs - k) % pairs) * 2 + 1 - core
        landed(wrows(s * depth + plane * half, half), fwd_recv.at[s])
        landed(wrows(s * depth + (1 - plane) * half, half), last_recv.at[s])

    keys = dot(normed[...], wbuf[1]).astype(jnp.bfloat16)
    values = dot(normed[...], wbuf[2]).astype(jnp.bfloat16)
    out.relay(3)
    part = normed[pl.ds(pl.multiple_of(core * qrows, qrows), qrows), :]
    own_queries = (dot(part, wbuf[0]) * 0.125).astype(jnp.bfloat16)
    low = lax.broadcasted_iota(jnp.int32, (qrows, 128), 1) < 64
    outs = []
    for h in range(2):
        masked = jnp.where(low if h == 0 else jnp.logical_not(low), own_queries, jnp.zeros_like(own_queries))
        scores = dot_nt(masked, keys)
        powers = jnp.exp(scores - jnp.max(scores, axis=-1, keepdims=True))
        total = jnp.sum(powers, axis=-1, keepdims=True)
        outs.append(dot((powers / total).astype(jnp.bfloat16), values))
    att_all[pair, pl.ds(pl.multiple_of(core * qrows, qrows), qrows), :] = jnp.where(low, outs[0], outs[1]).astype(jnp.bfloat16)

    def att_slot(s):
        return att_all.at[s // 2, pl.ds(pl.multiple_of((s % 2) * qrows, qrows), qrows), :]

    att = DirectGather(me, att_slot, att_slot(me), att_send, att_recv)
    att.begin()
    out.across()
    pre_tile(3)
    att.relay()
    att.across()
    out.collect()
    out.finish()
    att.finish()

    attended = jnp.concatenate([att_all[p] for p in range(pairs)], axis=1)
    decoded = (lat_all[...].astype(jnp.float32) + dot(attended, wout_all[...])).astype(jnp.bfloat16)
    dec_all[...] = decoded
    dec_ref[...] = dec_all[pl.ds(pl.multiple_of(me * rows, rows), rows), :]
    normed[...] = norm_rows(decoded.astype(jnp.float32), gcross_ref[...]).astype(jnp.bfloat16)
    for load in loads[1:]:
        load.wait()
    cross_keys = dot(normed[...], wkv_ref[0]).astype(jnp.bfloat16).T
    cross_values = dot(normed[...], wkv_ref[1]).astype(jnp.bfloat16)
    zero = jnp.zeros((64, many), jnp.bfloat16)
    for p in range(pairs):
        kbd[p, :64, :many] = cross_keys[128 * p : 128 * p + 64, :]
        kbd[p, :64, many:] = zero
        kbd[p, 64:, :many] = zero
        kbd[p, 64:, many:] = cross_keys[128 * p + 64 : 128 * p + 128, :]
        vext[p, :, :128] = cross_values[:, 128 * p : 128 * p + 128]
        vext[p, :, 128:] = jnp.ones((many, 128), jnp.bfloat16)

    def post_tile(t, carry):
        at = pl.ds(pl.multiple_of(t * TILE, TILE), TILE)
        left = lax.broadcasted_iota(jnp.int32, (TILE, 128), 1) < 64
        for p in range(pairs):
            scores = dot(queries[at, 128 * p : 128 * p + 128], kbd[p])
            parts = []
            for h in range(2):
                s = scores[:, many * h : many * (h + 1)]
                powers = jnp.exp(s - jnp.max(s, axis=-1, keepdims=True)).astype(jnp.bfloat16)
                blended = dot(powers, vext[p])
                parts.append(blended[:, :128] / blended[:, 128:])
            crossed[:, 128 * p : 128 * p + 128] = jnp.where(left, parts[0], parts[1]).astype(jnp.bfloat16)
        joined = embedded[at, :] + dot(crossed[...], wback_ref[...])
        head_in = norm_rows(joined, ghead_ref[...]).astype(jnp.bfloat16)
        hidden = gelu(dot(head_in, whidden_ref[...])).astype(jnp.bfloat16)
        sdf_ref[:, at] = dot_nt(wsdf_ref[...].reshape(1, -1), hidden)
        return carry

    lax.fori_loop(0, PTS_DEV // TILE, post_tile, 0)

    for copy in copies:
        copy.wait_send()
    lat.drain()
    out.drain()
    att.drain()


def shards_kernel(
    n, latents, gain_self, w_qkv, w_out, gain_cross, w_kv, w_embed, gain_point,
    w_query, w_back, gain_head, w_hidden, w_sdf,
):
    rows, width = latents.shape
    many = rows * n
    vmem = pl.BlockSpec(memory_space=pltpu.VMEM)
    anywhere = pl.BlockSpec(memory_space=pl.ANY)
    dma = pltpu.SemaphoreType.DMA
    bf16 = jnp.bfloat16
    decoded, sdf = pl.pallas_call(
        functools.partial(whole_kernel, n),
        out_shape=(
            jax.ShapeDtypeStruct((rows, width), bf16),
            jax.ShapeDtypeStruct((1, PTS_DEV), jnp.float32),
        ),
        in_specs=[vmem] * 9 + [anywhere] * 4,
        out_specs=(vmem,) * 2,
        scratch_shapes=[
            pltpu.VMEM((many, width), bf16),
            pltpu.VMEM((n // 2, many, 128), bf16),
            pltpu.VMEM((width, width), bf16),
            pltpu.VMEM((3, width, 128), bf16),
            pltpu.VMEM((many, width), bf16),
            pltpu.VMEM(w_kv.shape, bf16),
            pltpu.VMEM(w_query.shape, bf16),
            pltpu.VMEM(w_back.shape, bf16),
            pltpu.VMEM(w_hidden.shape, bf16),
            pltpu.VMEM((PTS_DEV, width), jnp.float32),
            pltpu.VMEM((PTS_DEV, width), bf16),
            pltpu.VMEM((many, width), bf16),
            pltpu.VMEM((n // 2, 128, 2 * many), bf16),
            pltpu.VMEM((n // 2, many, 256), bf16),
            pltpu.VMEM((TILE, width), bf16),
            dma((26,)), dma((n,)), dma((26,)), dma((n,)), dma((26,)), dma((n,)),
            *[dma((n,))] * 12, dma, dma((4,)),
        ],
        compiler_params=pltpu.CompilerParams(collective_id=0, has_side_effects=True),
    )(
        latents, gain_self.reshape(1, -1), w_qkv, w_out, gain_cross.reshape(1, -1), w_embed,
        gain_point.reshape(1, -1), gain_head.reshape(1, -1), w_sdf, w_kv, w_query, w_back, w_hidden,
    )
    return decoded, sdf.reshape(PTS_DEV)


def attend(queries, keys, values):
    row_count, features = queries.shape
    key_count = keys.shape[0]
    head_dim = features // HEADS
    group_count = HEADS // 4
    head_queries = queries.reshape(row_count, group_count, 4, head_dim).transpose(1, 0, 2, 3)
    head_keys = keys.reshape(key_count, group_count, 4, head_dim).transpose(1, 0, 2, 3)
    head_values = values.reshape(key_count, group_count, 4, head_dim).transpose(1, 0, 2, 3)
    scaling = 1.0 / math.sqrt(head_dim)

    def per_group(block):
        group_query, group_keys, group_values = block
        scores = (
            jnp.einsum("rge,nge->grn", group_query, group_keys, preferred_element_type=jnp.float32)
            * scaling
        )
        highest = jnp.max(scores, axis=-1, keepdims=True)
        powers = jnp.exp(scores - highest)
        total = jnp.sum(powers, axis=-1, keepdims=True)
        weights = (powers / total).astype(jnp.bfloat16)
        blended = jnp.einsum(
            "grn,nge->rge", weights, group_values, preferred_element_type=jnp.float32
        )
        return blended.astype(jnp.bfloat16)

    result = lax.map(per_group, (head_queries, head_keys, head_values))
    return result.transpose(1, 0, 2, 3).reshape(row_count, features)


def point_features(numbers):
    cell_i = numbers // (GRID * GRID)
    cell_j = numbers // GRID % GRID
    cell_k = numbers % GRID
    cells = jnp.stack([cell_i, cell_j, cell_k], axis=1).astype(jnp.float32)
    coords = (2.0 * cells + 1.0) / GRID - 1.0
    freqs = 2.0 ** jnp.arange(FREQS, dtype=jnp.float32) * math.pi
    angles = (coords[:, :, None] * freqs[None, None, :]).reshape(numbers.shape[0], 3 * FREQS)
    return jnp.concatenate([coords, jnp.sin(angles), jnp.cos(angles)], axis=1).astype(jnp.bfloat16)


def shards_gathers(
    latents,
    gain_self,
    w_qkv,
    w_out,
    gain_cross,
    w_kv,
    w_embed,
    gain_point,
    w_query,
    w_back,
    gain_head,
    w_hidden,
    w_sdf,
):
    inputs = latents.astype(jnp.float32)
    normed = norm_rows(inputs, gain_self).astype(jnp.bfloat16)
    columns = normed
    qkv = jnp.einsum(
        "rd,sdc->src",
        columns,
        lax.all_gather(w_qkv, "query", axis=1, tiled=True),
        preferred_element_type=jnp.float32,
    ).astype(jnp.bfloat16)
    self_keys, self_values = (
        lax.all_gather(qkv[1], "query", axis=0, tiled=True),
        lax.all_gather(qkv[2], "query", axis=0, tiled=True),
    )
    attended = attend(qkv[0], self_keys, self_values)
    columns = attended
    update = jnp.dot(
        columns,
        lax.all_gather(w_out, "query", axis=0, tiled=True),
        preferred_element_type=jnp.float32,
    )
    decoded = (inputs + update).astype(jnp.bfloat16)
    normed_two = norm_rows(decoded.astype(jnp.float32), gain_cross).astype(jnp.bfloat16)
    stacked = jnp.einsum(
        "rd,sdc->src",
        lax.all_gather(normed_two, "query", axis=0, tiled=True),
        w_kv,
        preferred_element_type=jnp.float32,
    ).astype(jnp.bfloat16)
    cross_keys, cross_values = (stacked[0], stacked[1])
    numbers = lax.axis_index("query") * PTS_DEV + jnp.arange(PTS_DEV, dtype=jnp.int32)
    features = point_features(numbers)
    embedded = jnp.dot(features, w_embed, preferred_element_type=jnp.float32)
    point_normed = norm_rows(embedded, gain_point).astype(jnp.bfloat16)
    point_query = jnp.dot(point_normed, w_query, preferred_element_type=jnp.float32).astype(
        jnp.bfloat16
    )
    crossed = attend(point_query, cross_keys, cross_values)
    joined = embedded + jnp.dot(crossed, w_back, preferred_element_type=jnp.float32)
    head_in = norm_rows(joined, gain_head).astype(jnp.bfloat16)
    hidden = jax.nn.gelu(jnp.dot(head_in, w_hidden, preferred_element_type=jnp.float32)).astype(
        jnp.bfloat16
    )
    sdf = jnp.dot(hidden, w_sdf, preferred_element_type=jnp.float32)
    return (decoded, sdf)


def solution(mesh):
    n = mesh.shape["query"]
    body = functools.partial(shards_kernel, n) if n == HEADS and mesh.shape["shape"] == 2 else shards_gathers
    return jax.shard_map(
        body,
        mesh=mesh,
        in_specs=(
            P(("shape", "query"), None),
            P(),
            P(None, "query", None),
            P("query", None),
            P(),
            P(),
            P(),
            P(),
            P(),
            P(),
            P(),
            P(),
            P(),
        ),
        out_specs=(P(("shape", "query"), None), P(("shape", "query"))),
        check_vma=False,
    )
```
